32 devices in a mesh: groups: 2 (over y), tensor: 8 (over z, core), rows: 2 (over x).
Axes of the slice: x: 2, y: 2, z: 4, core: 2. Of those that a mesh axis runs over, the one named last changes fastest.
Arguments:
- queries: bfloat16 [2048, 8192], P(('groups', 'tensor'), 'rows'), parts along dimension 0, may hold values from -32 to 32
- keyvals: bfloat16 [16384, 2048], P(('groups', 'tensor'), 'rows'), parts along dimension 0, may hold values from -6 to 6
- attending: int32 [128, 4], P(('groups', 'tensor')), parts along dimension 0, may hold values from 0 to 7, all different within a row; in each aligned block of 8 rows (0 to 7, 8 to 15, ...) at most 8 rows name the same one
- block_fill: int32 [128], P(('groups', 'tensor')), parts along dimension 0, may hold values from 1 to 128
- out_weight: bfloat16 [8192, 8192], P('rows', 'tensor'), may hold values from -0.0625 to 0.0625
Outputs:
- projected: bfloat16 [2048, 8192], P(('groups', 'rows'), 'tensor'), parts along dimension 0
The draws below stay inside these ranges and needn't reach their ends.
There are 2 independent parts, one for each index of `groups`. The reference program is written for one: setup_inputs(seed, part) draws one part's arguments, and reference() takes and returns one part's arrays. A program takes and returns all parts, laid end to end along the dimension named above; an argument that names none is the same for every part. Nothing has to cross between parts.
Inputs may be any that keep to these rules, and one draw needn't show every extreme that they name: `attending`: each row names 4 different query blocks; among the 8 rows of one index of tensor no query block is named more than 8 times, and every query block is named by some row.
All inputs are finite; a program needn't handle non-finite values.
Results may differ from the reference program's by a relative error of at most 0.0052.
Values may be sent and summed in bfloat16 or wider, within the bound.
No kernel may reach another device: no remote copies, remote signals or barrier semaphores. Data moves between devices by JAX's collectives and lax.ppermute only.
A program may use at most 128 MiB of HBM per device.

```python
import math
import jax
import jax.numpy as jnp
import numpy as np
from jax import lax

D = 8192
QUERY_HEADS = 64
KEY_VALUE_HEADS = 8
HEAD_WIDTH = 128
BLOCK_TOKENS = 128
TOP = 4
KB_DEV = 8
PACKED_KEYS = 8192
MICRO_QUERIES = 1024
NKB = 64
CAP = 8
N_TENSOR = 8


def draw_queries(key, part):
    noise_random_key = jax.random.fold_in(key, 11)
    final_result = jnp.clip(2.5 * jax.random.normal(noise_random_key, (MICRO_QUERIES, KEY_VALUE_HEADS, QUERY_HEADS // KEY_VALUE_HEADS, HEAD_WIDTH), jnp.float32), -15.0, 15.0)
    return final_result.reshape(MICRO_QUERIES, QUERY_HEADS * HEAD_WIDTH).astype(jnp.bfloat16)


def draw_keyvals(key, part):
    noise_random_key = jax.random.fold_in(key, 21)
    final_result = jnp.clip(jax.random.normal(noise_random_key, (PACKED_KEYS, KEY_VALUE_HEADS, 2, HEAD_WIDTH), jnp.float32), -6.0, 6.0)
    return final_result.reshape(PACKED_KEYS, KEY_VALUE_HEADS * 2 * HEAD_WIDTH).astype(jnp.bfloat16)


def with_ends(values, rng, least, top_value):
    index_at = [jax.random.randint(jax.random.fold_in(rng, axis), (), 0, length) for axis, length in enumerate(values.shape)]
    longest = values.shape.index(max(values.shape))
    neighbour = index_at[:longest] + [(index_at[longest] + 1) % values.shape[longest]] + index_at[longest + 1:]
    return values.at[tuple(index_at)].set(least).at[tuple(neighbour)].set(top_value)


def block_levels(rng, dims, pieces, low, largest):
    factor_of = 1.0
    for axis_at, parts in pieces:
        draws = jax.random.uniform(jax.random.fold_in(jax.random.fold_in(rng, 6), axis_at), (parts,), jnp.float32, low / len(pieces), largest / len(pieces))
        factor_of = factor_of * jnp.repeat(jnp.exp(draws), dims[axis_at] // parts).reshape((-1,) + (1,) * (len(dims) - 1 - axis_at))
    return factor_of


def deal_out(key, own, number, rows, amount, top, reach, lean):
    sequence = jax.random.permutation(key, amount)
    packed, ordinary = shares(amount, rows * top, reach, lean, True), shares(amount, rows * top, reach, lean, False)
    places = jnp.arange(amount)

    def named(tallies, offset_by):
        used = int((tallies > 0).sum())
        fixed = max(1, used // 4)
        passed = fixed + (places - fixed + offset_by * (used - fixed)) % max(1, amount - fixed)
        return jnp.zeros((amount,), jnp.int32).at[sequence[jnp.where(places < fixed, places, passed)]].set(jnp.asarray(tallies, jnp.int32))

    tallies = jnp.where(number % 4 == 0, named(packed, number // 4), named(ordinary, number - number // 4 - 1))
    mixed = jax.random.permutation(jax.random.fold_in(own, 3), amount)
    giver, sink = mixed[0:amount // 2 * 2:2], mixed[1:amount // 2 * 2:2]
    room = jnp.minimum(tallies[giver] - 1, reach - tallies[sink]) // 2
    room = jnp.where((giver == sequence[0]) | (sink == sequence[0]) | (tallies[sink] == 0), 0, jnp.maximum(room, 0))
    passed = jax.random.randint(jax.random.fold_in(own, 4), (amount // 2,), 0, 1 << 20) % (room + 1)
    tallies = tallies.at[giver].add(-passed).at[sink].add(passed)
    labels = jnp.searchsorted(jnp.cumsum(tallies), jnp.arange(rows * top), side="right").astype(jnp.int32)
    grid = labels.reshape(top, rows).T
    grid = grid[jax.random.permutation(jax.random.fold_in(own, 1), rows)]
    offset_by = jax.random.randint(jax.random.fold_in(own, 2), (rows, 1), 0, top)
    return jnp.take_along_axis(grid, (jnp.arange(top)[None, :] + offset_by) % top, axis=1)


def shares(number_of, total, bound, skew, full):
    portions = [(1 << 20) // math.isqrt(standing ** skew) + 1 for standing in range(1, number_of + 1)]
    largest = bound if full else min(bound, max(-(-total // number_of), total * portions[0] // sum(portions)))
    least = 1 if total - largest >= number_of - 1 else 0
    counts, surplus = [largest] + [least] * (number_of - 1), total - largest - least * (number_of - 1)
    while surplus > 0:
        movable = [i for i in range(1, number_of) if counts[i] < largest] or [i for i in range(1, number_of) if counts[i] < bound]
        mass, left = sum([portions[i] for i in movable]), surplus
        for i in movable:
            extra = min(bound - counts[i], max(1, left * portions[i] // mass), surplus)
            counts[i] = counts[i] + extra
            surplus = surplus - extra
    return np.array(counts)


def noise(stream_key, shape, scale, bound, cuts=(), kind=jnp.bfloat16):
    factor_of = block_levels(stream_key, shape, cuts, -0.22, 0.18) if cuts else 1.0
    array = jax.random.normal(stream_key, shape, jnp.float32) * scale * factor_of
    return jnp.minimum(jnp.maximum(array, -bound), bound).astype(kind)


def setup_inputs(seed: int = 0, part: int = 0) -> dict:
    key_list = jax.random.split(jax.random.key(seed), 6)
    part_splits = jax.random.split(jax.random.fold_in(key_list[5], part), 6)
    queries = draw_queries(jax.random.fold_in(jax.random.fold_in(key_list[5], part), 71), part)
    keyvals = draw_keyvals(jax.random.fold_in(jax.random.fold_in(key_list[5], part), 71), part)
    attending_keys = jax.random.split(jax.random.fold_in(part_splits[2], 1), NKB // KB_DEV)
    attending_turns = jax.random.permutation(jax.random.fold_in(part_splits[2], 3), NKB // KB_DEV)
    attending = jax.vmap(lambda own, number: deal_out(jax.random.fold_in(part_splits[2], 2), own, number, KB_DEV, N_TENSOR, TOP, CAP, 2))(attending_keys, attending_turns).reshape((NKB, TOP))
    block_fill = with_ends(jax.random.randint(part_splits[3], (NKB,), 1, BLOCK_TOKENS + 1), jax.random.fold_in(part_splits[3], 1), 1, BLOCK_TOKENS).astype(jnp.int32)
    out_weight = noise(key_list[4], (QUERY_HEADS * HEAD_WIDTH, D), (QUERY_HEADS * HEAD_WIDTH) ** -0.5, 0.0625, ((0, 2), (1, 8)))
    return dict(queries=queries, keyvals=keyvals, attending=attending, block_fill=block_fill, out_weight=out_weight)


masked_low = -1e+30

def reference(queries, keyvals, attending, block_fill, out_weight):
    query_block_rows = MICRO_QUERIES // BLOCK_TOKENS
    query_group_width = QUERY_HEADS // KEY_VALUE_HEADS
    score_scale = 1.0 / math.sqrt(HEAD_WIDTH)
    listed = jnp.any(attending[:, :, None] == jnp.arange(query_block_rows, dtype=jnp.int32)[None, None, :], axis=1)
    token_ok = jnp.arange(BLOCK_TOKENS, dtype=jnp.int32)[None, :] < block_fill[:, None]
    reshaped_tensor = keyvals.reshape(PACKED_KEYS, KEY_VALUE_HEADS, 2, HEAD_WIDTH)
    key_heads = jnp.transpose(reshaped_tensor[:, :, 0, :], (1, 0, 2))
    value_heads = jnp.transpose(reshaped_tensor[:, :, 1, :], (1, 0, 2))
    query_partition = jnp.transpose(queries.reshape(query_block_rows, BLOCK_TOKENS, KEY_VALUE_HEADS, query_group_width, HEAD_WIDTH), (0, 2, 1, 3, 4))
    query_partition = query_partition.reshape(query_block_rows, KEY_VALUE_HEADS, BLOCK_TOKENS * query_group_width, HEAD_WIDTH)

    def one_head(q_rows, key_rows, value_rows, visible):
        scores = jnp.dot(q_rows, key_rows.T, preferred_element_type=jnp.float32) * score_scale
        highest = lax.optimization_barrier(jnp.max(jnp.where(visible[None, :], scores, masked_low), axis=1, keepdims=True))
        probs = jnp.where(visible[None, :], jnp.exp(scores - highest), 0.0)
        totals = lax.optimization_barrier(jnp.sum(probs, axis=1, keepdims=True))
        summed = jnp.dot(probs.astype(jnp.bfloat16), value_rows, preferred_element_type=jnp.float32)
        return (summed / totals).astype(jnp.bfloat16)

    def one_block(block_args):
        head_queries, listed_row = block_args
        visible = (listed_row[:, None] & token_ok).reshape(PACKED_KEYS)
        return lax.map(lambda head_args: one_head(head_args[0], head_args[1], head_args[2], visible), (head_queries, key_heads, value_heads))
    attended_output = lax.map(one_block, (query_partition, listed.T))
    attended_output = jnp.transpose(attended_output.reshape(query_block_rows, KEY_VALUE_HEADS, BLOCK_TOKENS, query_group_width, HEAD_WIDTH), (0, 2, 1, 3, 4))
    attended_output = attended_output.reshape(MICRO_QUERIES, QUERY_HEADS * HEAD_WIDTH)
    return jnp.dot(attended_output, out_weight, preferred_element_type=jnp.float32).astype(jnp.bfloat16)
```

```python
import functools
import math

import jax
import jax.numpy as jnp
from jax import lax
from jax.experimental import pallas as pl
from jax.experimental.pallas import tpu as pltpu
from jax.sharding import PartitionSpec as P

HEAD_WIDTH = 128
BLOCK_TOKENS = 128
masked_low = -1e30
exp2_scale = math.log2(math.e) / math.sqrt(HEAD_WIDTH)
key_group = 4
meta_rows = 16


slab_rows = 512


def head_scores(q_heads, key_heads):
    scores = jnp.einsum("hrd,hkd->hrk", q_heads, key_heads, preferred_element_type=jnp.float32)
    return scores * (1.0 / math.sqrt(HEAD_WIDTH))


def fold_keys(q_heads, key_heads, value_heads, visible):
    head_count = key_heads.shape[0]
    row_count = q_heads.shape[1]
    key_count = key_heads.shape[1]
    slab_size = math.gcd(key_count, slab_rows)
    slab_count = key_count // slab_size
    keys_split = jnp.transpose(
        key_heads.reshape(head_count, slab_count, slab_size, HEAD_WIDTH), (1, 0, 2, 3)
    )
    values_split = jnp.transpose(
        value_heads.reshape(head_count, slab_count, slab_size, HEAD_WIDTH), (1, 0, 2, 3)
    )
    visible_split = visible.reshape(slab_count, slab_size)

    def find_top(current, pieces):
        scores = head_scores(q_heads, pieces[0])
        return (
            jnp.maximum(
                current, jnp.max(jnp.where(pieces[1][None, None, :], scores, masked_low), axis=2)
            ),
            None,
        )

    highest, unused = lax.scan(
        find_top,
        jnp.full((head_count, row_count), masked_low, jnp.float32),
        (keys_split, visible_split),
    )

    def accumulate(current, pieces):
        totals, summed = current
        scores = head_scores(q_heads, pieces[0])
        probs = jnp.where(pieces[2][None, None, :], jnp.exp(scores - highest[..., None]), 0.0)
        totals = totals + jnp.sum(probs, axis=2)
        summed = summed + jnp.einsum(
            "hrk,hkd->hrd",
            probs.astype(jnp.bfloat16),
            pieces[1],
            preferred_element_type=jnp.float32,
        )
        return ((totals, summed), None)

    start_state = (
        jnp.zeros((head_count, row_count), jnp.float32),
        jnp.zeros((head_count, row_count, HEAD_WIDTH), jnp.float32),
    )
    final_state, unused = lax.scan(
        accumulate, start_state, (keys_split, values_split, visible_split)
    )
    return final_state[1] / final_state[0][..., None]


def split_heads(kv_rows):
    key_count = kv_rows.shape[0]
    head_count = kv_rows.shape[1] // (2 * HEAD_WIDTH)
    reshaped_tensor = kv_rows.reshape(key_count, head_count, 2, HEAD_WIDTH)
    return (
        jnp.transpose(reshaped_tensor[:, :, 0, :], (1, 0, 2)),
        jnp.transpose(reshaped_tensor[:, :, 1, :], (1, 0, 2)),
    )


def gathered_shards(queries, keyvals, attending, block_fill, out_weight):
    q_len = queries.shape[0]
    head_count = keyvals.shape[1] // (2 * HEAD_WIDTH)
    query_group_width = queries.shape[1] // (HEAD_WIDTH * head_count)
    row_count = q_len * query_group_width
    positions = jnp.arange(BLOCK_TOKENS, dtype=jnp.int32)
    token_ok = positions[None, :] < block_fill[:, None]
    q_heads = jnp.transpose(
        queries.reshape(q_len, head_count, query_group_width, HEAD_WIDTH), (1, 0, 2, 3)
    ).reshape(head_count, row_count, HEAD_WIDTH)
    powers = jnp.sum(jnp.power(2, attending), axis=1).astype(jnp.int32)
    visible_bits = jnp.where(token_ok, powers[:, None], 0).reshape(keyvals.shape[0])
    my_bit = jnp.power(2, lax.axis_index("tensor"))
    all_rows, all_bits = (
        lax.all_gather(keyvals, "tensor", axis=0, tiled=True),
        lax.all_gather(visible_bits, "tensor", axis=0, tiled=True),
    )
    visible = all_bits // my_bit % 2 == 1
    key_heads, value_heads = split_heads(all_rows)
    merged = fold_keys(q_heads, key_heads, value_heads, visible)
    attended_output = jnp.transpose(
        merged.reshape(head_count, q_len, query_group_width, HEAD_WIDTH), (1, 0, 2, 3)
    )
    attended_output = attended_output.reshape(
        q_len, head_count * query_group_width * HEAD_WIDTH
    ).astype(jnp.bfloat16)
    terms = jnp.dot(
        lax.all_gather(attended_output, "tensor", axis=0, tiled=True),
        out_weight,
        preferred_element_type=jnp.float32,
    )
    return lax.psum_scatter(terms, "rows", scatter_dimension=0, tiled=True).astype(jnp.bfloat16)


def attend_kernel(heads, slots, tab, cnt, qb, qs, q_ref, *refs):
    kv_in = refs[:slots]
    o_ref, kv, s_all, acc, tops, q_rows, sems = refs[slots:]
    step = pl.program_id(0)
    width = HEAD_WIDTH
    per_slot = kv_in[0].shape[0]

    @pl.when(step == 0)
    def _():
        copies = [
            pltpu.make_async_copy(kv_in[i], kv.at[pl.ds(per_slot * i, per_slot)], sems.at[i])
            for i in range(slots)
        ]
        for copy in copies:
            copy.start()
        for copy in copies:
            copy.wait()

    block = qb[step]
    groups = (cnt[block] + (key_group - 1)) // key_group
    for h in range(heads):
        q_rows[h] = q_ref[0, :, h * width : (h + 1) * width]
    tops[...] = jnp.full_like(tops, masked_low)
    acc[...] = jnp.zeros_like(acc)
    lane = lax.broadcasted_iota(jnp.int32, (1, BLOCK_TOKENS), 1)

    def find(j, carry):
        entries = [tab[block, j * key_group + p] for p in range(key_group)]
        keys = jnp.concatenate([kv[e // 256, :, :width] for e in entries], axis=0)
        hidden = jnp.concatenate(
            [jnp.where(lane < e % 256, 0.0, masked_low) for e in entries], axis=1
        )
        for h in range(heads):
            scores = lax.dot_general(
                q_rows[h], keys, (((1,), (1,)), ((), ())), preferred_element_type=jnp.float32
            )
            scores = scores + hidden
            s_all[j, h] = scores
            top = tops[h]
            for p in range(key_group):
                top = jnp.maximum(top, scores[:, p * BLOCK_TOKENS : (p + 1) * BLOCK_TOKENS])
            tops[h] = top
        return carry

    lax.fori_loop(0, groups, find, 0)
    for h in range(heads):
        top = jnp.max(tops[h], axis=1, keepdims=True) * exp2_scale
        tops[h] = jnp.broadcast_to(top, tops.shape[1:])

    def gather(j, carry):
        entries = [tab[block, j * key_group + p] for p in range(key_group)]
        values = jnp.concatenate([kv[e // 256, :, width:] for e in entries], axis=0)
        values = jnp.concatenate([values, jnp.ones_like(values)], axis=1)
        for h in range(heads):
            top = tops[h]
            probs = jnp.concatenate(
                [
                    jnp.exp2(
                        s_all[j, h, :, p * BLOCK_TOKENS : (p + 1) * BLOCK_TOKENS] * exp2_scale
                        - top
                    ).astype(jnp.bfloat16)
                    for p in range(key_group)
                ],
                axis=1,
            )
            acc[h] += jnp.dot(probs, values, preferred_element_type=jnp.float32)
        return carry

    lax.fori_loop(0, groups, gather, 0)
    for h in range(heads):
        o_ref[:, h * width : (h + 1) * width] = (acc[h, :, :width] / acc[h, :, width:]).astype(
            o_ref.dtype
        )


def attend(tab, cnt, qb, qs, q_all, kv_slots):
    count = qb.shape[0]
    slots = len(kv_slots)
    width = q_all.shape[2]
    heads = width // HEAD_WIDTH
    blocks = tab.shape[1]
    per_slot = kv_slots[0].shape[0]
    keys = blocks * BLOCK_TOKENS
    tasks = blocks * 4 // 8 * count
    return pl.pallas_call(
        functools.partial(attend_kernel, heads, slots),
        out_shape=jax.ShapeDtypeStruct((count * BLOCK_TOKENS, width), jnp.bfloat16),
        grid_spec=pltpu.PrefetchScalarGridSpec(
            num_scalar_prefetch=4,
            grid=(count,),
            in_specs=[
                pl.BlockSpec(
                    (1, BLOCK_TOKENS, width), lambda i, tab, cnt, qb, qs: (qs[i], 0, 0)
                )
            ]
            + [pl.BlockSpec(memory_space=pl.ANY)] * slots,
            out_specs=pl.BlockSpec((BLOCK_TOKENS, width), lambda i, *_: (i, 0)),
            scratch_shapes=[
                pltpu.VMEM((blocks, BLOCK_TOKENS, 2 * HEAD_WIDTH), jnp.bfloat16),
                pltpu.VMEM(
                    (blocks // key_group, heads, BLOCK_TOKENS, key_group * BLOCK_TOKENS),
                    jnp.float32,
                ),
                pltpu.VMEM((heads, BLOCK_TOKENS, 2 * HEAD_WIDTH), jnp.float32),
                pltpu.VMEM((heads, BLOCK_TOKENS, HEAD_WIDTH), jnp.float32),
                pltpu.VMEM((heads, BLOCK_TOKENS, HEAD_WIDTH), jnp.bfloat16),
                pltpu.SemaphoreType.DMA((slots,)),
            ],
        ),
        compiler_params=pltpu.CompilerParams(vmem_limit_bytes=40 << 20),
        cost_estimate=pl.CostEstimate(
            flops=tasks * heads * 4 * BLOCK_TOKENS * BLOCK_TOKENS * HEAD_WIDTH * 6,
            bytes_accessed=keys * 512,
            transcendentals=tasks * heads * BLOCK_TOKENS * BLOCK_TOKENS,
        ),
        name="attend",
    )(tab, cnt, qb, qs, q_all, *kv_slots)


def project_kernel(pieces, with_sum, at, *refs):
    parts = refs[:pieces]
    w_ref = refs[pieces]
    o_ref = refs[-1]
    depth = parts[0].shape[1]
    total = None
    for i in range(pieces):
        rows = pl.ds(pl.multiple_of(at[i] * depth, depth), depth)
        term = jnp.dot(parts[i][...], w_ref[rows, :], preferred_element_type=jnp.float32)
        total = term if total is None else total + term
    if with_sum:
        total = total + refs[pieces + 1][...].astype(jnp.float32)
    o_ref[...] = total.astype(o_ref.dtype)


def project(at, parts, weight, other=None):
    pieces = len(parts)
    rows, depth = parts[0].shape
    columns = weight.shape[1]
    tile = 256
    specs = [pl.BlockSpec((rows, depth), lambda j, at: (0, 0))] * pieces
    specs.append(pl.BlockSpec((weight.shape[0], tile), lambda j, at: (0, j)))
    operands = [at, *parts, weight]
    if other is not None:
        specs.append(pl.BlockSpec((rows, tile), lambda j, at: (0, j)))
        operands.append(other)
    return pl.pallas_call(
        functools.partial(project_kernel, pieces, other is not None),
        out_shape=jax.ShapeDtypeStruct((rows, columns), jnp.bfloat16),
        grid_spec=pltpu.PrefetchScalarGridSpec(
            num_scalar_prefetch=1,
            grid=(columns // tile,),
            in_specs=specs,
            out_specs=pl.BlockSpec((rows, tile), lambda j, at: (0, j)),
        ),
        compiler_params=pltpu.CompilerParams(vmem_limit_bytes=32 << 20),
        cost_estimate=pl.CostEstimate(
            flops=2 * rows * weight.shape[0] * columns,
            bytes_accessed=2 * (weight.size + rows * weight.shape[0] + rows * columns),
            transcendentals=0,
        ),
        name="project",
    )(*operands)


def apart(k):
    return [(i, i ^ k) for i in range(8)]


def key_lists(meta, blocks):
    slots = meta.shape[0]
    naming = meta[:, : 8 * 4].reshape(slots * 8, 4)
    fill = meta[:, 8 * 4 : 8 * 5].reshape(slots * 8)
    listed = jnp.any(naming[None] == jnp.arange(blocks, dtype=jnp.int32)[:, None, None], axis=2)
    ones = listed.astype(jnp.int32)
    total = slots * 8
    place = jnp.arange(total, dtype=jnp.int32)
    before = jnp.sum(jnp.where(place[None, :] < place[:, None], ones[:, None, :], 0), axis=2)
    entry = place * 256 + fill
    tab = jnp.sum(
        jnp.where(
            listed[:, :, None] & (before[:, :, None] == place[None, None, :]),
            entry[None, :, None],
            0,
        ),
        axis=1,
    )
    return tab, jnp.sum(ones, axis=1)


def exchanged_shards(queries, keyvals, attending, block_fill, out_weight):
    t = lax.axis_index("tensor")
    z, core = t // 2, t % 2
    row = lax.axis_index("rows")
    chips = 4
    swap = functools.partial(lax.ppermute, axis_name="tensor", perm=apart(1))
    q_len = queries.shape[0]
    wide = queries.shape[1] // (2 * chips)

    meta = jnp.concatenate([attending.reshape(-1), block_fill]).astype(jnp.bfloat16)
    meta = jnp.pad(meta[None, :], ((0, meta_rows - 1), (0, wide - meta.shape[0])))
    q_split = jnp.transpose(queries.reshape(q_len, chips, 2, wide), (1, 2, 0, 3))
    q_split = jnp.concatenate(
        [q_split, jnp.broadcast_to(meta, (chips, 2, meta_rows, wide))], axis=2
    )
    kv_split = jnp.transpose(keyvals.reshape(keyvals.shape[0], chips, 2 * HEAD_WIDTH), (1, 0, 2))

    def for_chip(array, at):
        return lax.dynamic_index_in_dim(array, at, 0, keepdims=False)

    q_come = [for_chip(q_split, z)] + [
        lax.ppermute(for_chip(q_split, z ^ k), "tensor", apart(2 * k)) for k in range(1, chips)
    ]
    kv_mine = [for_chip(kv_split, z)] + [
        lax.ppermute(for_chip(kv_split, z ^ k), "tensor", apart(2 * k)) for k in range(1, chips)
    ]
    q_come = jnp.stack(q_come)
    q_mine = lax.dynamic_index_in_dim(q_come, core, 1, keepdims=False)
    q_other = swap(lax.dynamic_index_in_dim(q_come, 1 - core, 1, keepdims=False))
    q_all = jnp.stack([q_mine, q_other], axis=1).reshape(2 * chips, q_len + meta_rows, wide)
    kv_slots = []
    for k in range(chips):
        kv_slots += [kv_mine[k], swap(kv_mine[k])]
    kv_slots = [a.reshape(-1, BLOCK_TOKENS, 2 * HEAD_WIDTH) for a in kv_slots]
    tab, cnt = key_lists(q_all[:, q_len, :64].astype(jnp.int32), 2 * chips)

    far = jnp.where(z < 2, 2, 1)
    chip_of = jnp.stack([z, z ^ 1, far, far ^ 1])
    at = jnp.concatenate([2 * chip_of + core, 2 * chip_of + 1 - core]).astype(jnp.int32)
    middle = (z == 1) | (z == 2)

    def chunk(chip):
        pair = 2 * chip + jnp.arange(2, dtype=jnp.int32)
        slot = 2 * (chip ^ z) + (jnp.arange(2, dtype=jnp.int32) ^ core)
        mine = attend(tab, cnt, pair.astype(jnp.int32), slot.astype(jnp.int32), q_all, kv_slots)
        near = lax.ppermute(mine, "tensor", apart(2))
        two = jnp.stack([mine, near])
        across = lax.ppermute(two, "tensor", [(2, 4), (3, 5), (4, 2), (5, 3)])
        out = lax.ppermute(across, "tensor", [(2, 0), (3, 1), (4, 6), (5, 7)])
        rest = jnp.where(middle, across, out)
        four = [mine, near, rest[0], rest[1]]
        two_s, rest_s = swap(two), swap(rest)
        return four + [two_s[0], two_s[1], rest_s[0], rest_s[1]]

    theirs = []
    for i in range(2):
        term = project(at, chunk(2 * (1 - row) + i), out_weight)
        theirs.append(lax.ppermute(term, "rows", [(0, 1), (1, 0)]))
    ours = [project(at, chunk(2 * row + i), out_weight, theirs[i]) for i in range(2)]
    return jnp.concatenate(ours, axis=0)


def solution(mesh):
    def shards(queries, keyvals, attending, block_fill, out_weight):
        split = (
            mesh.shape["tensor"] == 8
            and mesh.shape["rows"] == 2
            and keyvals.shape[1] == 4 * 2 * HEAD_WIDTH
            and queries.shape[0] == BLOCK_TOKENS
            and keyvals.shape[0] == 8 * BLOCK_TOKENS
        )
        form = exchanged_shards if split else gathered_shards
        return form(queries, keyvals, attending, block_fill, out_weight)

    return jax.shard_map(
        shards,
        mesh=mesh,
        in_specs=(
            P(("groups", "tensor"), "rows"),
            P(("groups", "tensor"), "rows"),
            P(("groups", "tensor"), None),
            P(("groups", "tensor")),
            P("rows", "tensor"),
        ),
        out_specs=P(("groups", "rows"), "tensor"),
        check_vma=False,
    )
```

```python
import functools
import math

import jax
import jax.numpy as jnp
from jax import lax
from jax.experimental import pallas as pl
from jax.experimental.pallas import tpu as pltpu
from jax.sharding import PartitionSpec as P

HEAD_WIDTH = 128
BLOCK_TOKENS = 128
masked_low = -1e30
exp2_scale = math.log2(math.e) / math.sqrt(HEAD_WIDTH)
key_group = 4
meta_rows = 16
share = 16


slab_rows = 512


def head_scores(q_heads, key_heads):
    scores = jnp.einsum("hrd,hkd->hrk", q_heads, key_heads, preferred_element_type=jnp.float32)
    return scores * (1.0 / math.sqrt(HEAD_WIDTH))


def fold_keys(q_heads, key_heads, value_heads, visible):
    head_count = key_heads.shape[0]
    row_count = q_heads.shape[1]
    key_count = key_heads.shape[1]
    slab_size = math.gcd(key_count, slab_rows)
    slab_count = key_count // slab_size
    keys_split = jnp.transpose(
        key_heads.reshape(head_count, slab_count, slab_size, HEAD_WIDTH), (1, 0, 2, 3)
    )
    values_split = jnp.transpose(
        value_heads.reshape(head_count, slab_count, slab_size, HEAD_WIDTH), (1, 0, 2, 3)
    )
    visible_split = visible.reshape(slab_count, slab_size)

    def find_top(current, pieces):
        scores = head_scores(q_heads, pieces[0])
        return (
            jnp.maximum(
                current, jnp.max(jnp.where(pieces[1][None, None, :], scores, masked_low), axis=2)
            ),
            None,
        )

    highest, unused = lax.scan(
        find_top,
        jnp.full((head_count, row_count), masked_low, jnp.float32),
        (keys_split, visible_split),
    )

    def accumulate(current, pieces):
        totals, summed = current
        scores = head_scores(q_heads, pieces[0])
        probs = jnp.where(pieces[2][None, None, :], jnp.exp(scores - highest[..., None]), 0.0)
        totals = totals + jnp.sum(probs, axis=2)
        summed = summed + jnp.einsum(
            "hrk,hkd->hrd",
            probs.astype(jnp.bfloat16),
            pieces[1],
            preferred_element_type=jnp.float32,
        )
        return ((totals, summed), None)

    start_state = (
        jnp.zeros((head_count, row_count), jnp.float32),
        jnp.zeros((head_count, row_count, HEAD_WIDTH), jnp.float32),
    )
    final_state, unused = lax.scan(
        accumulate, start_state, (keys_split, values_split, visible_split)
    )
    return final_state[1] / final_state[0][..., None]


def split_heads(kv_rows):
    key_count = kv_rows.shape[0]
    head_count = kv_rows.shape[1] // (2 * HEAD_WIDTH)
    reshaped_tensor = kv_rows.reshape(key_count, head_count, 2, HEAD_WIDTH)
    return (
        jnp.transpose(reshaped_tensor[:, :, 0, :], (1, 0, 2)),
        jnp.transpose(reshaped_tensor[:, :, 1, :], (1, 0, 2)),
    )


def gathered_shards(queries, keyvals, attending, block_fill, out_weight):
    q_len = queries.shape[0]
    head_count = keyvals.shape[1] // (2 * HEAD_WIDTH)
    query_group_width = queries.shape[1] // (HEAD_WIDTH * head_count)
    row_count = q_len * query_group_width
    positions = jnp.arange(BLOCK_TOKENS, dtype=jnp.int32)
    token_ok = positions[None, :] < block_fill[:, None]
    q_heads = jnp.transpose(
        queries.reshape(q_len, head_count, query_group_width, HEAD_WIDTH), (1, 0, 2, 3)
    ).reshape(head_count, row_count, HEAD_WIDTH)
    powers = jnp.sum(jnp.power(2, attending), axis=1).astype(jnp.int32)
    visible_bits = jnp.where(token_ok, powers[:, None], 0).reshape(keyvals.shape[0])
    my_bit = jnp.power(2, lax.axis_index("tensor"))
    all_rows, all_bits = (
        lax.all_gather(keyvals, "tensor", axis=0, tiled=True),
        lax.all_gather(visible_bits, "tensor", axis=0, tiled=True),
    )
    visible = all_bits // my_bit % 2 == 1
    key_heads, value_heads = split_heads(all_rows)
    merged = fold_keys(q_heads, key_heads, value_heads, visible)
    attended_output = jnp.transpose(
        merged.reshape(head_count, q_len, query_group_width, HEAD_WIDTH), (1, 0, 2, 3)
    )
    attended_output = attended_output.reshape(
        q_len, head_count * query_group_width * HEAD_WIDTH
    ).astype(jnp.bfloat16)
    terms = jnp.dot(
        lax.all_gather(attended_output, "tensor", axis=0, tiled=True),
        out_weight,
        preferred_element_type=jnp.float32,
    )
    return lax.psum_scatter(terms, "rows", scatter_dimension=0, tiled=True).astype(jnp.bfloat16)


def attend_kernel(first, last, heads, tab, cnt, qb, qk, qp, qa_ref, qs_ref, kv_a, kv_b, *refs):
    if first:
        acc_in = top_in = None
    else:
        acc_in, top_in, *refs = refs
    if last:
        o_ref, kv, s_all, tops, q_rows, sems, acc = refs
    else:
        acc_out, top_out, kv, s_all, tops, q_rows, sems = refs
        acc = acc_out.at[0]
    step = pl.program_id(0)
    width = HEAD_WIDTH
    half = kv_a.shape[0]

    @pl.when(step == 0)
    def _():
        copies = [
            pltpu.make_async_copy(source, kv.at[pl.ds(half * i, half)], sems.at[i])
            for i, source in enumerate((kv_a, kv_b))
        ]
        for copy in copies:
            copy.start()
        for copy in copies:
            copy.wait()

    for parity, q_ref in enumerate((qa_ref, qs_ref)):

        @pl.when(qp[step] == parity)
        def _():
            for h in range(heads):
                q_rows[h * BLOCK_TOKENS : (h + 1) * BLOCK_TOKENS] = q_ref[
                    0, :, h * width : (h + 1) * width
                ]

    block = qb[step]
    groups = (cnt[block] + (key_group - 1)) // key_group
    tops[...] = jnp.full_like(tops, masked_low)
    lane = lax.broadcasted_iota(jnp.int32, (1, BLOCK_TOKENS), 1)

    def find(j, carry):
        top = tops[...]
        for p in range(0, key_group, 2):
            entries = [tab[block, j * key_group + p + i] for i in range(2)]
            keys = jnp.concatenate([kv[e // 256, :, :width] for e in entries], axis=0)
            hidden = jnp.concatenate(
                [jnp.where(lane < e % 256, 0.0, masked_low) for e in entries], axis=1
            )
            scores = lax.dot_general(
                q_rows[...], keys, (((1,), (1,)), ((), ())), preferred_element_type=jnp.float32
            )
            scores = scores + hidden
            s_all[j, :, p * BLOCK_TOKENS : (p + 2) * BLOCK_TOKENS] = scores
            top = jnp.maximum(top, jnp.maximum(scores[:, :width], scores[:, width:]))
        tops[...] = top
        return carry

    lax.fori_loop(0, groups, find, 0)
    top = jnp.max(tops[...], axis=1, keepdims=True) * exp2_scale
    top = jnp.broadcast_to(top, tops.shape)
    if first:
        acc[...] = jnp.zeros(acc.shape, jnp.float32)
    else:
        before = top_in[0]
        top = jnp.maximum(top, before)
        fade = jnp.exp2(before - top)
        acc[:, :width] = acc_in[0, :, :width] * fade
        acc[:, width:] = acc_in[0, :, width:] * fade
    tops[...] = top
    if not last:
        top_out[0] = top

    def gather(j, carry):
        entries = [tab[block, j * key_group + p] for p in range(key_group)]
        values = jnp.concatenate([kv[e // 256, :, width:] for e in entries], axis=0)
        values = jnp.concatenate([values, jnp.ones_like(values)], axis=1)
        probs = jnp.concatenate(
            [
                jnp.exp2(
                    s_all[j, :, p * BLOCK_TOKENS : (p + 1) * BLOCK_TOKENS] * exp2_scale - tops[...]
                ).astype(jnp.bfloat16)
                for p in range(key_group)
            ],
            axis=1,
        )
        acc[...] += jnp.dot(probs, values, preferred_element_type=jnp.float32)
        return carry

    lax.fori_loop(0, groups, gather, 0)
    if last:
        for h in range(heads):
            rows = slice(h * BLOCK_TOKENS, (h + 1) * BLOCK_TOKENS)
            o_ref[:, h * width : (h + 1) * width] = (acc[rows, :width] / acc[rows, width:]).astype(
                o_ref.dtype
            )


def attend(lists, at, q_own, q_swap, kv_own, kv_swap, state=None, last=False):
    tab, cnt = lists
    qb, qk, qp = at
    count = qb.shape[0]
    width = q_own.shape[2]
    heads = width // HEAD_WIDTH
    rows = heads * BLOCK_TOKENS
    blocks = tab.shape[1]
    q_spec = pl.BlockSpec((1, BLOCK_TOKENS, width), lambda i, tab, cnt, qb, qk, qp: (qk[i], 0, 0))
    acc_spec = pl.BlockSpec((1, rows, 2 * HEAD_WIDTH), lambda i, tab, cnt, qb, qk, qp: (qb[i], 0, 0))
    top_spec = pl.BlockSpec((1, rows, HEAD_WIDTH), lambda i, tab, cnt, qb, qk, qp: (qb[i], 0, 0))
    scratch = [
        pltpu.VMEM((blocks, BLOCK_TOKENS, 2 * HEAD_WIDTH), jnp.bfloat16),
        pltpu.VMEM((blocks // key_group, rows, key_group * BLOCK_TOKENS), jnp.float32),
        pltpu.VMEM((rows, HEAD_WIDTH), jnp.float32),
        pltpu.VMEM((rows, HEAD_WIDTH), jnp.bfloat16),
        pltpu.SemaphoreType.DMA((2,)),
    ]
    if last:
        out_shape = jax.ShapeDtypeStruct((count * BLOCK_TOKENS, width), jnp.bfloat16)
        out_specs = pl.BlockSpec((BLOCK_TOKENS, width), lambda i, *_: (i, 0))
        scratch.append(pltpu.VMEM((rows, 2 * HEAD_WIDTH), jnp.float32))
    else:
        out_shape = (
            jax.ShapeDtypeStruct((count, rows, 2 * HEAD_WIDTH), jnp.float32),
            jax.ShapeDtypeStruct((count, rows, HEAD_WIDTH), jnp.float32),
        )
        out_specs = (acc_spec, top_spec)
    shape = (kv_own.shape[0] // BLOCK_TOKENS, BLOCK_TOKENS, kv_own.shape[1])
    state = () if state is None else state
    work = count * blocks // 2 * rows * BLOCK_TOKENS
    return pl.pallas_call(
        functools.partial(attend_kernel, not state, last, heads),
        out_shape=out_shape,
        grid_spec=pltpu.PrefetchScalarGridSpec(
            num_scalar_prefetch=5,
            grid=(count,),
            in_specs=[q_spec, q_spec]
            + [pl.BlockSpec(memory_space=pl.ANY)] * 2
            + [acc_spec, top_spec][: len(state)],
            out_specs=out_specs,
            scratch_shapes=scratch,
        ),
        compiler_params=pltpu.CompilerParams(vmem_limit_bytes=24 << 20),
        cost_estimate=pl.CostEstimate(
            flops=work * 4 * HEAD_WIDTH * 4, bytes_accessed=work // 8, transcendentals=work
        ),
        name="attend",
    )(
        tab,
        cnt,
        qb,
        qk,
        qp,
        q_own,
        q_swap,
        kv_own.reshape(shape),
        kv_swap.reshape(shape),
        *state,
    )


def project_kernel(at, middle, mine, near, in_a, in_b, out_a, out_b, w_own, w_swap, *refs):
    own_ref, other_ref, one, two, sems = refs
    column = pl.program_id(0)
    depth = mine.shape[1]

    @pl.when(column == 0)
    def _():
        for flag, pair in ((1, (in_a, in_b)), (0, (out_a, out_b))):

            @pl.when(middle[0] == flag)
            def _():
                copies = [
                    pltpu.make_async_copy(pair[0], one, sems.at[0]),
                    pltpu.make_async_copy(pair[1], two, sems.at[1]),
                ]
                for copy in copies:
                    copy.start()
                for copy in copies:
                    copy.wait()

    for own, (w_ref, o_ref) in enumerate(((w_swap, other_ref), (w_own, own_ref))):
        total = None
        for i, part in enumerate((mine, near, one, two)):
            place = at[4 * own + i]
            rows = pl.ds(pl.multiple_of(place * depth, depth), depth)
            term = jnp.dot(part[...], w_ref[rows, :], preferred_element_type=jnp.float32)
            total = term if total is None else total + term
        o_ref[...] = total.astype(o_ref.dtype)


def project(at, middle, parts, w_own, w_swap):
    rows, depth = parts[0].shape
    columns = w_own.shape[1]
    tile = 256
    whole = pl.BlockSpec((rows, depth), lambda j, *_: (0, 0))
    strip = pl.BlockSpec((rows, tile), lambda j, *_: (0, j))
    result = jax.ShapeDtypeStruct((rows, columns), jnp.bfloat16)
    return pl.pallas_call(
        project_kernel,
        out_shape=(jax.ShapeDtypeStruct((rows, columns), jnp.float32), result),
        grid_spec=pltpu.PrefetchScalarGridSpec(
            num_scalar_prefetch=2,
            grid=(columns // tile,),
            in_specs=[whole, whole]
            + [pl.BlockSpec(memory_space=pl.ANY)] * 4
            + [
                pl.BlockSpec((w_own.shape[0], tile), lambda j, *_: (0, j)),
                pl.BlockSpec((w_swap.shape[0], tile), lambda j, *_: (0, j)),
            ],
            out_specs=(strip, strip),
            scratch_shapes=[
                pltpu.VMEM((rows, depth), jnp.bfloat16),
                pltpu.VMEM((rows, depth), jnp.bfloat16),
                pltpu.SemaphoreType.DMA((2,)),
            ],
        ),
        compiler_params=pltpu.CompilerParams(vmem_limit_bytes=24 << 20),
        cost_estimate=pl.CostEstimate(
            flops=2 * rows * 4 * depth * 2 * columns,
            bytes_accessed=2 * (8 * depth * columns + 6 * rows * depth + 3 * rows * columns),
            transcendentals=0,
        ),
        name="project",
    )(at, middle, *parts, w_own, w_swap)


def apart(k):
    return [(i, i ^ k) for i in range(8)]


def key_lists(meta, blocks):
    chips = meta.shape[0]
    naming = meta[:, :, : 8 * 4].reshape(chips, share, 4)
    fill = meta[:, :, 8 * 4 : 8 * 5].reshape(chips, share)
    wanted = jnp.arange(blocks, dtype=jnp.int32)[None, :, None, None]
    listed = jnp.any(naming[:, None] == wanted, axis=3)
    ones = listed.astype(jnp.int32)
    place = jnp.arange(share, dtype=jnp.int32)
    before = jnp.sum(jnp.where(place[None, :] < place[:, None], ones[:, :, None, :], 0), axis=3)
    entry = place * 256 + fill
    tab = jnp.sum(
        jnp.where(
            listed[..., None] & (before[..., None] == place),
            entry[:, None, :, None],
            0,
        ),
        axis=2,
    )
    return tab, jnp.sum(ones, axis=2)


def exchanged_shards(queries, keyvals, attending, block_fill, out_weight):
    t = lax.axis_index("tensor")
    z, core = t // 2, t % 2
    row = lax.axis_index("rows")
    chips = 4
    swap = functools.partial(lax.ppermute, axis_name="tensor", perm=apart(1))
    q_len = queries.shape[0]
    wide = queries.shape[1] // chips
    pair = 2 * HEAD_WIDTH

    meta = jnp.concatenate([attending.reshape(-1), block_fill]).astype(jnp.bfloat16)
    meta = jnp.pad(meta[None, :], ((0, meta_rows - 1), (0, wide // 2 - meta.shape[0])))
    meta = jnp.concatenate([meta, meta], axis=1)

    def q_for(chip):
        own = lax.dynamic_slice(queries, (0, chip * wide), (q_len, wide))
        return jnp.concatenate([own, meta], axis=0)

    def kv_for(chip):
        return lax.dynamic_slice(keyvals, (0, chip * pair), (keyvals.shape[0], pair))

    q_come = [q_for(z)]
    for k in range(1, chips):
        q_come.append(lax.ppermute(q_for(z ^ k), "tensor", apart(2 * k)))
    kv_own = [kv_for(z)]
    for k in range(1, chips):
        kv_own.append(lax.ppermute(kv_for(z ^ k), "tensor", apart(2 * k)))
    kv_swap = [swap(a) for a in kv_own]

    def columns_of(which):
        size = (q_len + meta_rows, wide // 2)
        return jnp.stack(
            [lax.dynamic_slice(a, (0, which * (wide // 2)), size) for a in q_come]
        )

    q_own = columns_of(core)
    q_swap = swap(columns_of(1 - core))
    notes = jnp.stack([q_own[:, q_len, :64], q_swap[:, q_len, :64]], axis=1)
    tab, cnt = key_lists(notes.astype(jnp.int32), 2 * chips)

    def places(blocks):
        blocks = blocks.astype(jnp.int32)
        return (
            blocks,
            ((blocks // 2) ^ z).astype(jnp.int32),
            ((blocks % 2) ^ core).astype(jnp.int32),
        )

    everything = places(jnp.arange(2 * chips, dtype=jnp.int32))
    state = None
    for k in range(chips - 1):
        state = attend((tab[k], cnt[k]), everything, q_own, q_swap, kv_own[k], kv_swap[k], state)

    depth = wide // 2
    w_split = out_weight.reshape(chips, 2, depth, out_weight.shape[1])
    w_swap = swap(lax.dynamic_index_in_dim(w_split, 1 - core, 1, keepdims=False))
    w_swap = w_swap.reshape(chips * depth, out_weight.shape[1])
    far = jnp.where(z < 2, 2, 1)
    chip_of = jnp.stack([z, z ^ 1, far, far ^ 1])
    at = jnp.concatenate([chip_of, 2 * chip_of + core]).astype(jnp.int32)
    middle = ((z == 1) | (z == 2)).astype(jnp.int32).reshape(1)
    across = [(2, 4), (3, 5), (4, 2), (5, 3)]
    outward = [(2, 0), (3, 1), (4, 6), (5, 7)]
    last = chips - 1

    def chunk(chip):
        pieces = places(2 * chip + jnp.arange(2, dtype=jnp.int32))
        mine = attend(
            (tab[last], cnt[last]),
            pieces,
            q_own,
            q_swap,
            kv_own[last],
            kv_swap[last],
            state,
            last=True,
        )
        near = lax.ppermute(mine, "tensor", apart(2))
        in_a = lax.ppermute(mine, "tensor", across)
        in_b = lax.ppermute(near, "tensor", across)
        out_a = lax.ppermute(in_a, "tensor", outward)
        out_b = lax.ppermute(in_b, "tensor", outward)
        own, other = project(
            at, middle, (mine, near, in_a, in_b, out_a, out_b), out_weight, w_swap
        )
        return own, swap(other)

    theirs = []
    for i in range(2):
        own, come = chunk(2 * (1 - row) + i)
        term = (own + come.astype(jnp.float32)).astype(jnp.bfloat16)
        theirs.append(lax.ppermute(term, "rows", [(0, 1), (1, 0)]))
    ours = []
    for i in range(2):
        own, come = chunk(2 * row + i)
        ours.append(own + come.astype(jnp.float32) + theirs[i].astype(jnp.float32))
    return jnp.concatenate(ours, axis=0).astype(jnp.bfloat16)


def solution(mesh):
    def shards(queries, keyvals, attending, block_fill, out_weight):
        split = (
            mesh.shape["tensor"] == 8
            and mesh.shape["rows"] == 2
            and keyvals.shape[1] == 4 * 2 * HEAD_WIDTH
            and queries.shape[0] == BLOCK_TOKENS
            and keyvals.shape[0] == 8 * BLOCK_TOKENS
        )
        form = exchanged_shards if split else gathered_shards
        return form(queries, keyvals, attending, block_fill, out_weight)

    return jax.shard_map(
        shards,
        mesh=mesh,
        in_specs=(
            P(("groups", "tensor"), "rows"),
            P(("groups", "tensor"), "rows"),
            P(("groups", "tensor"), None),
            P(("groups", "tensor")),
            P("rows", "tensor"),
        ),
        out_specs=P(("groups", "rows"), "tensor"),
        check_vma=False,
    )
```

```python
import functools
import math

import jax
import jax.numpy as jnp
from jax import lax
from jax.experimental import pallas as pl
from jax.experimental.pallas import tpu as pltpu
from jax.sharding import PartitionSpec as P


HEAD_WIDTH = 128
BLOCK_TOKENS = 128
masked_low = -1e30
exp2_scale = math.log2(math.e) / math.sqrt(HEAD_WIDTH)
key_group = 4
meta_rows = 16
share = 16


slab_rows = 512


def head_scores(q_heads, key_heads):
    scores = jnp.einsum("hrd,hkd->hrk", q_heads, key_heads, preferred_element_type=jnp.float32)
    return scores * (1.0 / math.sqrt(HEAD_WIDTH))


def fold_keys(q_heads, key_heads, value_heads, visible):
    head_count = key_heads.shape[0]
    row_count = q_heads.shape[1]
    key_count = key_heads.shape[1]
    slab_size = math.gcd(key_count, slab_rows)
    slab_count = key_count // slab_size
    keys_split = jnp.transpose(
        key_heads.reshape(head_count, slab_count, slab_size, HEAD_WIDTH), (1, 0, 2, 3)
    )
    values_split = jnp.transpose(
        value_heads.reshape(head_count, slab_count, slab_size, HEAD_WIDTH), (1, 0, 2, 3)
    )
    visible_split = visible.reshape(slab_count, slab_size)

    def find_top(current, pieces):
        scores = head_scores(q_heads, pieces[0])
        return (
            jnp.maximum(
                current, jnp.max(jnp.where(pieces[1][None, None, :], scores, masked_low), axis=2)
            ),
            None,
        )

    highest, unused = lax.scan(
        find_top,
        jnp.full((head_count, row_count), masked_low, jnp.float32),
        (keys_split, visible_split),
    )

    def accumulate(current, pieces):
        totals, summed = current
        scores = head_scores(q_heads, pieces[0])
        probs = jnp.where(pieces[2][None, None, :], jnp.exp(scores - highest[..., None]), 0.0)
        totals = totals + jnp.sum(probs, axis=2)
        summed = summed + jnp.einsum(
            "hrk,hkd->hrd",
            probs.astype(jnp.bfloat16),
            pieces[1],
            preferred_element_type=jnp.float32,
        )
        return ((totals, summed), None)

    start_state = (
        jnp.zeros((head_count, row_count), jnp.float32),
        jnp.zeros((head_count, row_count, HEAD_WIDTH), jnp.float32),
    )
    final_state, unused = lax.scan(
        accumulate, start_state, (keys_split, values_split, visible_split)
    )
    return final_state[1] / final_state[0][..., None]


def split_heads(kv_rows):
    key_count = kv_rows.shape[0]
    head_count = kv_rows.shape[1] // (2 * HEAD_WIDTH)
    reshaped_tensor = kv_rows.reshape(key_count, head_count, 2, HEAD_WIDTH)
    return (
        jnp.transpose(reshaped_tensor[:, :, 0, :], (1, 0, 2)),
        jnp.transpose(reshaped_tensor[:, :, 1, :], (1, 0, 2)),
    )


def gathered_shards(queries, keyvals, attending, block_fill, out_weight):
    q_len = queries.shape[0]
    head_count = keyvals.shape[1] // (2 * HEAD_WIDTH)
    query_group_width = queries.shape[1] // (HEAD_WIDTH * head_count)
    row_count = q_len * query_group_width
    positions = jnp.arange(BLOCK_TOKENS, dtype=jnp.int32)
    token_ok = positions[None, :] < block_fill[:, None]
    q_heads = jnp.transpose(
        queries.reshape(q_len, head_count, query_group_width, HEAD_WIDTH), (1, 0, 2, 3)
    ).reshape(head_count, row_count, HEAD_WIDTH)
    powers = jnp.sum(jnp.power(2, attending), axis=1).astype(jnp.int32)
    visible_bits = jnp.where(token_ok, powers[:, None], 0).reshape(keyvals.shape[0])
    my_bit = jnp.power(2, lax.axis_index("tensor"))
    all_rows, all_bits = (
        lax.all_gather(keyvals, "tensor", axis=0, tiled=True),
        lax.all_gather(visible_bits, "tensor", axis=0, tiled=True),
    )
    visible = all_bits // my_bit % 2 == 1
    key_heads, value_heads = split_heads(all_rows)
    merged = fold_keys(q_heads, key_heads, value_heads, visible)
    attended_output = jnp.transpose(
        merged.reshape(head_count, q_len, query_group_width, HEAD_WIDTH), (1, 0, 2, 3)
    )
    attended_output = attended_output.reshape(
        q_len, head_count * query_group_width * HEAD_WIDTH
    ).astype(jnp.bfloat16)
    terms = jnp.dot(
        lax.all_gather(attended_output, "tensor", axis=0, tiled=True),
        out_weight,
        preferred_element_type=jnp.float32,
    )
    return lax.psum_scatter(terms, "rows", scatter_dimension=0, tiled=True).astype(jnp.bfloat16)


def attend_kernel(first, last, heads, held, tab, cnt, qb, qk, qp, *refs):
    q_refs, (kv_a, kv_b, *refs) = refs[:4], refs[4:]
    if held:
        acc_in, top_in, *refs = refs
    if last:
        o_ref, kv, s_all, tops, q_rows, sems, acc = refs
    else:
        acc_out, top_out, kv, s_all, tops, q_rows, sems = refs
        acc = acc_out.at[0]
    step = pl.program_id(0)
    width = HEAD_WIDTH
    half = kv_a.shape[0]

    @pl.when(step == 0)
    def _():
        copies = [
            pltpu.make_async_copy(source, kv.at[pl.ds(half * i, half)], sems.at[i])
            for i, source in enumerate((kv_a, kv_b))
        ]
        for copy in copies:
            copy.start()
        for copy in copies:
            copy.wait()

    for which, q_ref in enumerate(q_refs):

        @pl.when(qp[step] == which)
        def _():
            for h in range(heads):
                q_rows[h * BLOCK_TOKENS : (h + 1) * BLOCK_TOKENS] = q_ref[
                    0, :, h * width : (h + 1) * width
                ]

    block = qb[step]
    groups = (cnt[block] + (key_group - 1)) // key_group
    tops[...] = jnp.full_like(tops, masked_low)
    lane = lax.broadcasted_iota(jnp.int32, (1, BLOCK_TOKENS), 1)

    def find(j, carry):
        top = tops[...]
        for p in range(0, key_group, 2):
            entries = [tab[block, j * key_group + p + i] for i in range(2)]
            keys = jnp.concatenate([kv[e // 256, :, :width] for e in entries], axis=0)
            hidden = jnp.concatenate(
                [jnp.where(lane < e % 256, 0.0, masked_low) for e in entries], axis=1
            )
            scores = lax.dot_general(
                q_rows[...], keys, (((1,), (1,)), ((), ())), preferred_element_type=jnp.float32
            )
            scores = scores + hidden
            s_all[j, :, p * BLOCK_TOKENS : (p + 2) * BLOCK_TOKENS] = scores
            top = jnp.maximum(top, jnp.maximum(scores[:, :width], scores[:, width:]))
        tops[...] = top
        return carry

    lax.fori_loop(0, groups, find, 0)
    top = jnp.max(tops[...], axis=1, keepdims=True) * exp2_scale
    top = jnp.broadcast_to(top, tops.shape)
    if first:
        acc[...] = jnp.zeros(acc.shape, jnp.float32)
    else:
        before = top_in[0]
        top = jnp.maximum(top, before)
        fade = jnp.exp2(before - top)
        acc[:, :width] = acc_in[0, :, :width] * fade
        acc[:, width:] = acc_in[0, :, width:] * fade
    tops[...] = top
    if not last:
        top_out[0] = top

    def gather(j, carry):
        entries = [tab[block, j * key_group + p] for p in range(key_group)]
        values = jnp.concatenate([kv[e // 256, :, width:] for e in entries], axis=0)
        values = jnp.concatenate([values, jnp.ones_like(values)], axis=1)
        probs = jnp.concatenate(
            [
                jnp.exp2(
                    s_all[j, :, p * BLOCK_TOKENS : (p + 1) * BLOCK_TOKENS] * exp2_scale - tops[...]
                ).astype(jnp.bfloat16)
                for p in range(key_group)
            ],
            axis=1,
        )
        acc[...] += jnp.dot(probs, values, preferred_element_type=jnp.float32)
        return carry

    lax.fori_loop(0, groups, gather, 0)
    if last:
        for h in range(heads):
            rows = slice(h * BLOCK_TOKENS, (h + 1) * BLOCK_TOKENS)
            o_ref[:, h * width : (h + 1) * width] = (acc[rows, :width] / acc[rows, width:]).astype(
                o_ref.dtype
            )


def attend(lists, at, q_four, kv_own, kv_swap, state=(), first=False, last=False):
    tab, cnt = lists
    qb, qk, qp = at
    count = qb.shape[0]
    width = q_four[0].shape[2]
    heads = width // HEAD_WIDTH
    rows = heads * BLOCK_TOKENS
    blocks = tab.shape[1]
    everyone = cnt.shape[0]
    q_spec = pl.BlockSpec((1, BLOCK_TOKENS, width), lambda i, tab, cnt, qb, qk, qp: (qk[i], 0, 0))
    acc_spec = pl.BlockSpec((1, rows, 2 * HEAD_WIDTH), lambda i, tab, cnt, qb, qk, qp: (qb[i], 0, 0))
    top_spec = pl.BlockSpec((1, rows, HEAD_WIDTH), lambda i, tab, cnt, qb, qk, qp: (qb[i], 0, 0))
    scratch = [
        pltpu.VMEM((blocks, BLOCK_TOKENS, 2 * HEAD_WIDTH), jnp.bfloat16),
        pltpu.VMEM((blocks // key_group, rows, key_group * BLOCK_TOKENS), jnp.float32),
        pltpu.VMEM((rows, HEAD_WIDTH), jnp.float32),
        pltpu.VMEM((rows, HEAD_WIDTH), jnp.bfloat16),
        pltpu.SemaphoreType.DMA((2,)),
    ]
    state_specs = [acc_spec, top_spec]
    if first:
        state_specs = [pl.BlockSpec(memory_space=pl.ANY)] * 2
    if last:
        out_shape = jax.ShapeDtypeStruct((count * BLOCK_TOKENS, width), jnp.bfloat16)
        out_specs = pl.BlockSpec((BLOCK_TOKENS, width), lambda i, *_: (i, 0))
        scratch.append(pltpu.VMEM((rows, 2 * HEAD_WIDTH), jnp.float32))
        aliases = {}
    else:
        out_shape = (
            jax.ShapeDtypeStruct((everyone, rows, 2 * HEAD_WIDTH), jnp.float32),
            jax.ShapeDtypeStruct((everyone, rows, HEAD_WIDTH), jnp.float32),
        )
        out_specs = (acc_spec, top_spec)
        aliases = {11 + i: i for i in range(len(state))}
    shape = (kv_own.shape[0] // BLOCK_TOKENS, BLOCK_TOKENS, kv_own.shape[1])
    work = count * blocks // 2 * rows * BLOCK_TOKENS
    return pl.pallas_call(
        functools.partial(attend_kernel, first, last, heads, bool(state)),
        out_shape=out_shape,
        grid_spec=pltpu.PrefetchScalarGridSpec(
            num_scalar_prefetch=5,
            grid=(count,),
            in_specs=[q_spec] * 4
            + [pl.BlockSpec(memory_space=pl.ANY)] * 2
            + state_specs[: len(state)],
            out_specs=out_specs,
            scratch_shapes=scratch,
        ),
        input_output_aliases=aliases,
        compiler_params=pltpu.CompilerParams(vmem_limit_bytes=60 << 20),
        cost_estimate=pl.CostEstimate(
            flops=work * 4 * HEAD_WIDTH * 4, bytes_accessed=work // 8, transcendentals=work
        ),
        name="attend",
    )(
        tab,
        cnt,
        qb,
        qk,
        qp,
        *q_four,
        kv_own.reshape(shape),
        kv_swap.reshape(shape),
        *state,
    )


def project_kernel(at, middle, mine, near, in_a, in_b, out_a, out_b, w_own, w_swap, *refs):
    own_ref, other_ref, one, two, sems = refs
    column = pl.program_id(0)

    @pl.when(column == 0)
    def _():
        for flag, pair in ((1, (in_a, in_b)), (0, (out_a, out_b))):

            @pl.when(middle[0] == flag)
            def _():
                copies = [
                    pltpu.make_async_copy(pair[0], one, sems.at[0]),
                    pltpu.make_async_copy(pair[1], two, sems.at[1]),
                ]
                for copy in copies:
                    copy.start()
                for copy in copies:
                    copy.wait()

    for w_ref, o_ref in ((w_swap, other_ref), (w_own, own_ref)):
        total = None
        for i, part in enumerate((mine, near, one, two)):
            term = jnp.dot(part[...], w_ref[at[i]], preferred_element_type=jnp.float32)
            total = term if total is None else total + term
        o_ref[...] = total.astype(o_ref.dtype)


def project(at, middle, parts, w_own, w_swap):
    rows, depth = parts[0].shape
    chips, _, columns = w_own.shape
    tile = 256
    whole = pl.BlockSpec((rows, depth), lambda j, *_: (0, 0))
    strip = pl.BlockSpec((rows, tile), lambda j, *_: (0, j))
    result = jax.ShapeDtypeStruct((rows, columns), jnp.bfloat16)
    return pl.pallas_call(
        project_kernel,
        out_shape=(jax.ShapeDtypeStruct((rows, columns), jnp.float32), result),
        grid_spec=pltpu.PrefetchScalarGridSpec(
            num_scalar_prefetch=2,
            grid=(columns // tile,),
            in_specs=[whole, whole]
            + [pl.BlockSpec(memory_space=pl.ANY)] * 4
            + [
                pl.BlockSpec((chips, depth, tile), lambda j, at, middle: (0, at[chips], j)),
                pl.BlockSpec((chips, depth, tile), lambda j, *_: (0, 0, j)),
            ],
            out_specs=(strip, strip),
            scratch_shapes=[
                pltpu.VMEM((rows, depth), jnp.bfloat16),
                pltpu.VMEM((rows, depth), jnp.bfloat16),
                pltpu.SemaphoreType.DMA((2,)),
            ],
        ),
        compiler_params=pltpu.CompilerParams(vmem_limit_bytes=60 << 20),
        cost_estimate=pl.CostEstimate(
            flops=2 * rows * 4 * depth * 2 * columns,
            bytes_accessed=2 * (8 * depth * columns + 6 * rows * depth + 3 * rows * columns),
            transcendentals=0,
        ),
        name="project",
    )(at, middle, *parts, w_own, w_swap)


def apart(k):
    return [(i, i ^ k) for i in range(8)]


def key_lists(meta, blocks):
    chips = meta.shape[0]
    naming = meta[:, :, : 8 * 4].reshape(chips, share, 4)
    fill = meta[:, :, 8 * 4 : 8 * 5].reshape(chips, share)
    wanted = jnp.arange(blocks, dtype=jnp.int32)[None, :, None, None]
    listed = jnp.any(naming[:, None] == wanted, axis=3)
    ones = listed.astype(jnp.int32)
    place = jnp.arange(share, dtype=jnp.int32)
    before = jnp.sum(jnp.where(place[None, :] < place[:, None], ones[:, :, None, :], 0), axis=3)
    entry = place * 256 + fill
    tab = jnp.sum(
        jnp.where(
            listed[..., None] & (before[..., None] == place),
            entry[:, None, :, None],
            0,
        ),
        axis=2,
    )
    return tab, jnp.sum(ones, axis=2)


def permute(array, perm, axis="tensor"):
    return lax.ppermute(array, axis, perm)


def exchanged_shards(queries, keyvals, attending, block_fill, out_weight):
    t = lax.axis_index("tensor")
    z, core = t // 2, t % 2
    row = lax.axis_index("rows")
    chips = 4
    q_len = queries.shape[0]
    wide = queries.shape[1] // chips
    depth = wide // 2
    pair = 2 * HEAD_WIDTH

    def swap(array):
        return permute(array, apart(1))

    meta = jnp.concatenate([attending.reshape(-1), block_fill]).astype(jnp.bfloat16)
    meta = jnp.pad(meta[None, :], ((0, meta_rows - 1), (0, depth - meta.shape[0])))
    meta = jnp.concatenate([meta, meta], axis=1)

    def q_for(chip):
        own = lax.dynamic_slice(queries, (0, chip * wide), (q_len, wide))
        return jnp.concatenate([own, meta], axis=0)

    def kv_for(chip):
        return lax.dynamic_slice(keyvals, (0, chip * pair), (keyvals.shape[0], pair))

    def columns_of(arrays, which):
        size = (q_len + meta_rows, depth)
        return jnp.stack([lax.dynamic_slice(a, (0, which * depth), size) for a in arrays])

    q_come = [q_for(z)]
    for k in range(1, chips):
        q_come.append(permute(q_for(z ^ k), apart(2 * k)))
    kv_own = [kv_for(z)]
    for k in range(1, chips):
        kv_own.append(permute(kv_for(z ^ k), apart(2 * k)))
    kv_swap = [swap(kv_own[k]) for k in range(chips)]

    near_own = columns_of(q_come[:2], core)
    near_swap = swap(columns_of(q_come[:2], 1 - core))
    far_own = columns_of(q_come[2:], core)
    far_swap = swap(columns_of(q_come[2:], 1 - core))
    q_four = [near_own, near_swap, far_own, far_swap]

    def lists_of(own, other):
        notes = jnp.stack([own[:, q_len, :64], other[:, q_len, :64]], axis=1)
        tab, cnt = key_lists(notes.astype(jnp.int32), 2 * chips)
        return [(tab[i], cnt[i]) for i in range(2)]

    lists = lists_of(near_own, near_swap)
    lists, far_notes = lax.optimization_barrier((lists, (far_own, far_swap)))
    lists = lists + lists_of(*far_notes)

    def places(blocks):
        blocks = blocks.astype(jnp.int32)
        k = (blocks // 2) ^ z
        which = 2 * (k // 2) + ((blocks % 2) ^ core)
        return blocks, (k % 2).astype(jnp.int32), which.astype(jnp.int32)

    four = jnp.arange(4, dtype=jnp.int32)
    near = places(4 * (z // 2) + four)
    far = places(4 * (1 - z // 2) + four)
    everything = places(jnp.arange(2 * chips, dtype=jnp.int32))
    q_near = q_four[:2] * 2
    state = attend(lists[0], near, q_near, kv_own[0], kv_swap[0], first=True)
    state = attend(lists[0], far, q_four, kv_own[0], kv_swap[0], state, first=True)
    state = attend(lists[1], everything, q_four, kv_own[1], kv_swap[1], state)
    state = attend(lists[2], everything, q_four, kv_own[2], kv_swap[2], state)

    w_split = out_weight.reshape(chips, 2, depth, out_weight.shape[1])
    w_swap = swap(lax.dynamic_index_in_dim(w_split, 1 - core, 1, keepdims=False))
    w_own = out_weight.reshape(chips, wide, out_weight.shape[1])
    far_chip = jnp.where(z < 2, 2, 1)
    chip_of = jnp.stack([z, z ^ 1, far_chip, far_chip ^ 1])
    at = jnp.concatenate([chip_of, core[None]]).astype(jnp.int32)
    middle = ((z == 1) | (z == 2)).astype(jnp.int32).reshape(1)
    across = [(2, 4), (3, 5), (4, 2), (5, 3)]
    outward = [(2, 0), (3, 1), (4, 6), (5, 7)]
    last = chips - 1

    def chunk(chip):
        pieces = places(2 * chip + jnp.arange(2, dtype=jnp.int32))
        mine = attend(lists[last], pieces, q_four, kv_own[last], kv_swap[last], state, last=True)
        beside = permute(mine, apart(2))
        in_a = permute(mine, across)
        in_b = permute(beside, across)
        out_a = permute(in_a, outward)
        out_b = permute(in_b, outward)
        own, other = project(at, middle, (mine, beside, in_a, in_b, out_a, out_b), w_own, w_swap)
        return own, swap(other)

    theirs = []
    for i in range(2):
        own, come = chunk(2 * (1 - row) + i)
        term = (own + come.astype(jnp.float32)).astype(jnp.bfloat16)
        theirs.append(permute(term, [(0, 1), (1, 0)], "rows"))
    ours = []
    for i in range(2):
        own, come = chunk(2 * row + i)
        ours.append(own + come.astype(jnp.float32) + theirs[i].astype(jnp.float32))
    return jnp.concatenate(ours, axis=0).astype(jnp.bfloat16)


def solution(mesh):
    tensor, rows = mesh.shape["tensor"], mesh.shape["rows"]

    def splits(queries, keyvals):
        return (
            tensor == 8
            and rows == 2
            and keyvals.shape[1] == 4 * 2 * HEAD_WIDTH
            and queries.shape[0] == BLOCK_TOKENS
            and keyvals.shape[0] == 8 * BLOCK_TOKENS
        )

    def shards(queries, keyvals, attending, block_fill, out_weight):
        form = exchanged_shards if splits(queries, keyvals) else gathered_shards
        return form(queries, keyvals, attending, block_fill, out_weight)

    return jax.shard_map(
        shards,
        mesh=mesh,
        in_specs=(
            P(("groups", "tensor"), "rows"),
            P(("groups", "tensor"), "rows"),
            P(("groups", "tensor"), None),
            P(("groups", "tensor")),
            P("rows", "tensor"),
        ),
        out_specs=P(("groups", "rows"), "tensor"),
        check_vma=False,
    )
```

```python
import functools
import math

import jax
import jax.numpy as jnp
from jax import lax
from jax.experimental import pallas as pl
from jax.experimental.pallas import tpu as pltpu
from jax.sharding import PartitionSpec as P


HEAD_WIDTH = 128
BLOCK_TOKENS = 128
masked_low = -1e30
exp2_scale = math.log2(math.e) / math.sqrt(HEAD_WIDTH)
key_group = 4
meta_rows = 16
share = 16
attend_vmem = 16 << 20


slab_rows = 512


def head_scores(q_heads, key_heads):
    scores = jnp.einsum("hrd,hkd->hrk", q_heads, key_heads, preferred_element_type=jnp.float32)
    return scores * (1.0 / math.sqrt(HEAD_WIDTH))


def fold_keys(q_heads, key_heads, value_heads, visible):
    head_count = key_heads.shape[0]
    row_count = q_heads.shape[1]
    key_count = key_heads.shape[1]
    slab_size = math.gcd(key_count, slab_rows)
    slab_count = key_count // slab_size
    keys_split = jnp.transpose(
        key_heads.reshape(head_count, slab_count, slab_size, HEAD_WIDTH), (1, 0, 2, 3)
    )
    values_split = jnp.transpose(
        value_heads.reshape(head_count, slab_count, slab_size, HEAD_WIDTH), (1, 0, 2, 3)
    )
    visible_split = visible.reshape(slab_count, slab_size)

    def find_top(current, pieces):
        scores = head_scores(q_heads, pieces[0])
        return (
            jnp.maximum(
                current, jnp.max(jnp.where(pieces[1][None, None, :], scores, masked_low), axis=2)
            ),
            None,
        )

    highest, unused = lax.scan(
        find_top,
        jnp.full((head_count, row_count), masked_low, jnp.float32),
        (keys_split, visible_split),
    )

    def accumulate(current, pieces):
        totals, summed = current
        scores = head_scores(q_heads, pieces[0])
        probs = jnp.where(pieces[2][None, None, :], jnp.exp(scores - highest[..., None]), 0.0)
        totals = totals + jnp.sum(probs, axis=2)
        summed = summed + jnp.einsum(
            "hrk,hkd->hrd",
            probs.astype(jnp.bfloat16),
            pieces[1],
            preferred_element_type=jnp.float32,
        )
        return ((totals, summed), None)

    start_state = (
        jnp.zeros((head_count, row_count), jnp.float32),
        jnp.zeros((head_count, row_count, HEAD_WIDTH), jnp.float32),
    )
    final_state, unused = lax.scan(
        accumulate, start_state, (keys_split, values_split, visible_split)
    )
    return final_state[1] / final_state[0][..., None]


def split_heads(kv_rows):
    key_count = kv_rows.shape[0]
    head_count = kv_rows.shape[1] // (2 * HEAD_WIDTH)
    reshaped_tensor = kv_rows.reshape(key_count, head_count, 2, HEAD_WIDTH)
    return (
        jnp.transpose(reshaped_tensor[:, :, 0, :], (1, 0, 2)),
        jnp.transpose(reshaped_tensor[:, :, 1, :], (1, 0, 2)),
    )


def gathered_shards(queries, keyvals, attending, block_fill, out_weight):
    q_len = queries.shape[0]
    head_count = keyvals.shape[1] // (2 * HEAD_WIDTH)
    query_group_width = queries.shape[1] // (HEAD_WIDTH * head_count)
    row_count = q_len * query_group_width
    positions = jnp.arange(BLOCK_TOKENS, dtype=jnp.int32)
    token_ok = positions[None, :] < block_fill[:, None]
    q_heads = jnp.transpose(
        queries.reshape(q_len, head_count, query_group_width, HEAD_WIDTH), (1, 0, 2, 3)
    ).reshape(head_count, row_count, HEAD_WIDTH)
    powers = jnp.sum(jnp.power(2, attending), axis=1).astype(jnp.int32)
    visible_bits = jnp.where(token_ok, powers[:, None], 0).reshape(keyvals.shape[0])
    my_bit = jnp.power(2, lax.axis_index("tensor"))
    all_rows, all_bits = (
        lax.all_gather(keyvals, "tensor", axis=0, tiled=True),
        lax.all_gather(visible_bits, "tensor", axis=0, tiled=True),
    )
    visible = all_bits // my_bit % 2 == 1
    key_heads, value_heads = split_heads(all_rows)
    merged = fold_keys(q_heads, key_heads, value_heads, visible)
    attended_output = jnp.transpose(
        merged.reshape(head_count, q_len, query_group_width, HEAD_WIDTH), (1, 0, 2, 3)
    )
    attended_output = attended_output.reshape(
        q_len, head_count * query_group_width * HEAD_WIDTH
    ).astype(jnp.bfloat16)
    terms = jnp.dot(
        lax.all_gather(attended_output, "tensor", axis=0, tiled=True),
        out_weight,
        preferred_element_type=jnp.float32,
    )
    return lax.psum_scatter(terms, "rows", scatter_dimension=0, tiled=True).astype(jnp.bfloat16)


def attend_kernel(chip, last, heads, tab, cnt, qb, qk, qp, *refs):
    q_refs, refs = refs[:2], refs[2:]
    chips = 4 if last else 1
    kv_refs, refs = refs[: 2 * chips], refs[2 * chips :]
    if last:
        acc_in, high_in, refs = refs[:chip], refs[chip : 2 * chip], refs[2 * chip :]
        o_ref, kv, q_rows, sems, acc, high, top = refs
    else:
        acc_out, high_out, kv, q_rows, sems = refs
        acc, high = acc_out.at[0], high_out.at[0]
    step = pl.program_id(0)
    width = HEAD_WIDTH
    half = kv_refs[0].shape[0]
    block = qb[step]
    lane = lax.broadcasted_iota(jnp.int32, (1, BLOCK_TOKENS), 1)

    def fetch(which):
        copies = [
            pltpu.make_async_copy(kv_refs[which * 2 + i], kv.at[pl.ds(half * i, half)], sems.at[i])
            for i in range(2)
        ]
        for copy in copies:
            copy.start()
        for copy in copies:
            copy.wait()

    def group_of(of, j):
        entries = [tab[of, block, j * key_group + p] for p in range(key_group)]
        hidden = [jnp.where(lane < e % 256, 0.0, masked_low) for e in entries]
        values = jnp.concatenate([kv[e // 256, :, width:] for e in entries], axis=0)
        values = jnp.concatenate([values, jnp.ones_like(values)], axis=1)
        keys = [kv[e // 256, :, :width] for e in entries]
        return keys, hidden, values

    def groups_of(of):
        return (cnt[of, block] + (key_group - 1)) // key_group

    def exponents(keys, hidden, i):
        pair = jnp.concatenate(keys[i : i + 2], axis=0)
        scores = lax.dot_general(
            q_rows[...], pair, (((1,), (1,)), ((), ())), preferred_element_type=jnp.float32
        )
        return scores * exp2_scale + jnp.concatenate(hidden[i : i + 2], axis=1)

    @pl.when(step == 0)
    def _():
        fetch(chips - 1)

    for which, q_ref in enumerate(q_refs):

        @pl.when(qp[step] == which)
        def _():
            for h in range(heads):
                q_rows[h * BLOCK_TOKENS : (h + 1) * BLOCK_TOKENS] = q_ref[
                    0, :, h * width : (h + 1) * width
                ]

    if last:
        acc[...] = functools.reduce(jnp.add, [a[0] for a in acc_in])
        high[...] = functools.reduce(jnp.maximum, [a[0] for a in high_in])
    else:
        acc[...] = jnp.zeros(acc.shape, jnp.float32)
        high[...] = jnp.full(high.shape, masked_low, jnp.float32)

    def fold(j, carry):
        keys, hidden, values = group_of(chip, j)
        probs = []
        highest = high[...]
        for i in range(0, key_group, 2):
            x = exponents(keys, hidden, i)
            for side in (x[:, :BLOCK_TOKENS], x[:, BLOCK_TOKENS:]):
                highest = jnp.maximum(highest, jnp.max(side.reshape(-1, 8, BLOCK_TOKENS), axis=0))
            probs.append(jnp.exp2(x).astype(jnp.bfloat16))
        high[...] = highest
        acc[...] += jnp.dot(
            jnp.concatenate(probs, axis=1), values, preferred_element_type=jnp.float32
        )
        return carry

    lax.fori_loop(0, groups_of(chip), fold, 0)
    if not last:
        return

    unsafe = (jnp.max(high[...]) > 100.0) | (jnp.min(acc[:, width:]) < 2.0**-80)

    @pl.when(unsafe)
    def _():
        acc[...] = jnp.zeros(acc.shape, jnp.float32)
        top[...] = jnp.full(top.shape, masked_low, jnp.float32)
        for of in range(chips):
            fetch(of)

            def fold_top(j, carry):
                keys, hidden, values = group_of(of, j)
                for i in range(0, key_group, 2):
                    x = exponents(keys, hidden, i)
                    before = top[...]
                    after = jnp.maximum(before, jnp.max(x, axis=1, keepdims=True))
                    fade = jnp.exp2(before - after)
                    top[...] = after
                    probs = jnp.exp2(x - jnp.concatenate([after, after], axis=1))
                    acc[...] = acc[...] * jnp.concatenate([fade, fade], axis=1) + jnp.dot(
                        probs.astype(jnp.bfloat16),
                        values[i * BLOCK_TOKENS : (i + 2) * BLOCK_TOKENS],
                        preferred_element_type=jnp.float32,
                    )
                return carry

            lax.fori_loop(0, groups_of(of), fold_top, 0)

    for h in range(heads):
        rows = slice(h * BLOCK_TOKENS, (h + 1) * BLOCK_TOKENS)
        o_ref[:, h * width : (h + 1) * width] = (acc[rows, :width] / acc[rows, width:]).astype(
            o_ref.dtype
        )


def attend(chip, lists, at, q_two, kv_refs, state=None):
    last = state is not None
    tab, cnt = lists
    qb, qk, qp = at
    count = qb.shape[0]
    width = q_two[0].shape[2]
    heads = width // HEAD_WIDTH
    rows = heads * BLOCK_TOKENS
    blocks = tab.shape[2]
    everyone = cnt.shape[1]
    q_spec = pl.BlockSpec((1, BLOCK_TOKENS, width), lambda i, tab, cnt, qb, qk, qp: (qk[i], 0, 0))
    acc_spec = pl.BlockSpec((1, rows, 2 * HEAD_WIDTH), lambda i, tab, cnt, qb, qk, qp: (qb[i], 0, 0))
    high_spec = pl.BlockSpec((1, 8, BLOCK_TOKENS), lambda i, tab, cnt, qb, qk, qp: (qb[i], 0, 0))
    scratch = [
        pltpu.VMEM((blocks, BLOCK_TOKENS, 2 * HEAD_WIDTH), jnp.bfloat16),
        pltpu.VMEM((rows, HEAD_WIDTH), jnp.bfloat16),
        pltpu.SemaphoreType.DMA((2,)),
    ]
    if last:
        out_shape = jax.ShapeDtypeStruct((count * BLOCK_TOKENS, width), jnp.bfloat16)
        out_specs = pl.BlockSpec((BLOCK_TOKENS, width), lambda i, *_: (i, 0))
        scratch += [
            pltpu.VMEM((rows, 2 * HEAD_WIDTH), jnp.float32),
            pltpu.VMEM((8, BLOCK_TOKENS), jnp.float32),
            pltpu.VMEM((rows, HEAD_WIDTH), jnp.float32),
        ]
    else:
        out_shape = (
            jax.ShapeDtypeStruct((everyone, rows, 2 * HEAD_WIDTH), jnp.float32),
            jax.ShapeDtypeStruct((everyone, 8, BLOCK_TOKENS), jnp.float32),
        )
        out_specs = (acc_spec, high_spec)
    shape = (kv_refs[0].shape[0] // BLOCK_TOKENS, BLOCK_TOKENS, kv_refs[0].shape[1])
    work = count * blocks // 2 * rows * BLOCK_TOKENS
    return pl.pallas_call(
        functools.partial(attend_kernel, chip, last, heads),
        out_shape=out_shape,
        grid_spec=pltpu.PrefetchScalarGridSpec(
            num_scalar_prefetch=5,
            grid=(count,),
            in_specs=[q_spec] * 2
            + [pl.BlockSpec(memory_space=pl.ANY)] * len(kv_refs)
            + ([acc_spec] * chip + [high_spec] * chip if last else []),
            out_specs=out_specs,
            scratch_shapes=scratch,
        ),
        compiler_params=pltpu.CompilerParams(vmem_limit_bytes=attend_vmem),
        cost_estimate=pl.CostEstimate(
            flops=work * 4 * HEAD_WIDTH * 4, bytes_accessed=work // 8, transcendentals=work
        ),
        name="attend",
    )(
        tab,
        cnt,
        qb,
        qk,
        qp,
        *q_two,
        *[a.reshape(shape) for a in kv_refs],
        *((*[a for a, _ in state], *[h for _, h in state]) if last else ()),
    )


def project_kernel(at, middle, mine, near, in_a, in_b, out_a, out_b, w_own, w_swap, *refs):
    own_ref, other_ref, one, two, sems = refs
    column = pl.program_id(0)

    @pl.when(column == 0)
    def _():
        for flag, pair in ((1, (in_a, in_b)), (0, (out_a, out_b))):

            @pl.when(middle[0] == flag)
            def _():
                copies = [
                    pltpu.make_async_copy(pair[0], one, sems.at[0]),
                    pltpu.make_async_copy(pair[1], two, sems.at[1]),
                ]
                for copy in copies:
                    copy.start()
                for copy in copies:
                    copy.wait()

    for w_ref, o_ref in ((w_swap, other_ref), (w_own, own_ref)):
        total = None
        for i, part in enumerate((mine, near, one, two)):
            term = jnp.dot(part[...], w_ref[at[i]], preferred_element_type=jnp.float32)
            total = term if total is None else total + term
        o_ref[...] = total.astype(o_ref.dtype)


def project(at, middle, parts, w_own, w_swap):
    rows, depth = parts[0].shape
    chips, _, columns = w_own.shape
    tile = 256
    whole = pl.BlockSpec((rows, depth), lambda j, *_: (0, 0))
    strip = pl.BlockSpec((rows, tile), lambda j, *_: (0, j))
    result = jax.ShapeDtypeStruct((rows, columns), jnp.bfloat16)
    return pl.pallas_call(
        project_kernel,
        out_shape=(jax.ShapeDtypeStruct((rows, columns), jnp.float32), result),
        grid_spec=pltpu.PrefetchScalarGridSpec(
            num_scalar_prefetch=2,
            grid=(columns // tile,),
            in_specs=[whole, whole]
            + [pl.BlockSpec(memory_space=pl.ANY)] * 4
            + [
                pl.BlockSpec((chips, depth, tile), lambda j, at, middle: (0, at[chips], j)),
                pl.BlockSpec((chips, depth, tile), lambda j, *_: (0, 0, j)),
            ],
            out_specs=(strip, strip),
            scratch_shapes=[
                pltpu.VMEM((rows, depth), jnp.bfloat16),
                pltpu.VMEM((rows, depth), jnp.bfloat16),
                pltpu.SemaphoreType.DMA((2,)),
            ],
        ),
        compiler_params=pltpu.CompilerParams(vmem_limit_bytes=60 << 20),
        cost_estimate=pl.CostEstimate(
            flops=2 * rows * 4 * depth * 2 * columns,
            bytes_accessed=2 * (8 * depth * columns + 6 * rows * depth + 3 * rows * columns),
            transcendentals=0,
        ),
        name="project",
    )(at, middle, *parts, w_own, w_swap)


def apart(k):
    return [(i, i ^ k) for i in range(8)]


def key_lists(meta, blocks):
    chips = meta.shape[0]
    naming = meta[:, :, : 8 * 4].reshape(chips, share, 4)
    fill = meta[:, :, 8 * 4 : 8 * 5].reshape(chips, share)
    wanted = jnp.arange(blocks, dtype=jnp.int32)[None, :, None, None]
    listed = jnp.any(naming[:, None] == wanted, axis=3)
    ones = listed.astype(jnp.int32)
    place = jnp.arange(share, dtype=jnp.int32)
    before = jnp.sum(jnp.where(place[None, :] < place[:, None], ones[:, :, None, :], 0), axis=3)
    entry = place * 256 + fill
    tab = jnp.sum(
        jnp.where(
            listed[..., None] & (before[..., None] == place),
            entry[:, None, :, None],
            0,
        ),
        axis=2,
    )
    return tab, jnp.sum(ones, axis=2)


def permute(array, perm, axis="tensor"):
    return lax.ppermute(array, axis, perm)


def exchanged_shards(queries, keyvals, attending, block_fill, out_weight):
    t = lax.axis_index("tensor")
    z, core = t // 2, t % 2
    row = lax.axis_index("rows")
    chips = 4
    q_len = queries.shape[0]
    wide = queries.shape[1] // chips
    depth = wide // 2
    pair = 2 * HEAD_WIDTH

    def swap(array):
        return permute(array, apart(1))

    meta = jnp.concatenate([attending.reshape(-1), block_fill]).astype(jnp.bfloat16)
    meta = jnp.pad(meta[None, :], ((0, meta_rows - 1), (0, depth - meta.shape[0])))
    meta = jnp.concatenate([meta, meta], axis=1)

    def q_for(chip):
        own = lax.dynamic_slice(queries, (0, chip * wide), (q_len, wide))
        return jnp.concatenate([own, meta], axis=0)

    def kv_for(chip):
        return lax.dynamic_slice(keyvals, (0, chip * pair), (keyvals.shape[0], pair))

    def columns_of(arrays, which):
        size = (q_len + meta_rows, depth)
        return jnp.stack([lax.dynamic_slice(a, (0, which * depth), size) for a in arrays])

    q_come = [q_for(z)]
    for k in range(1, chips):
        q_come.append(permute(q_for(z ^ k), apart(2 * k)))
    kv = []
    for k in range(chips):
        own = kv_for(z ^ k)
        if k:
            own = permute(own, apart(2 * k))
        kv.append((own, swap(own)))

    q_own = columns_of(q_come, core)
    q_swap = swap(columns_of(q_come, 1 - core))
    q_two = (q_own, q_swap)
    notes = jnp.stack([q_own[:, q_len, :64], q_swap[:, q_len, :64]], axis=1)
    lists = key_lists(notes.astype(jnp.int32), 2 * chips)

    def places(blocks):
        blocks = blocks.astype(jnp.int32)
        k = (blocks // 2) ^ z
        which = (blocks % 2) ^ core
        return blocks, k.astype(jnp.int32), which.astype(jnp.int32)

    everything = places(jnp.arange(2 * chips, dtype=jnp.int32))
    state = [attend(k, lists, everything, q_two, kv[k]) for k in range(chips - 1)]

    w_split = out_weight.reshape(chips, 2, depth, out_weight.shape[1])
    w_swap = swap(lax.dynamic_index_in_dim(w_split, 1 - core, 1, keepdims=False))
    w_own = out_weight.reshape(chips, wide, out_weight.shape[1])
    far_chip = jnp.where(z < 2, 2, 1)
    chip_of = jnp.stack([z, z ^ 1, far_chip, far_chip ^ 1])
    at = jnp.concatenate([chip_of, core[None]]).astype(jnp.int32)
    middle = ((z == 1) | (z == 2)).astype(jnp.int32).reshape(1)
    across = [(2, 4), (3, 5), (4, 2), (5, 3)]
    outward = [(2, 0), (3, 1), (4, 6), (5, 7)]
    last = chips - 1

    def chunk(chip):
        pieces = places(2 * chip + jnp.arange(2, dtype=jnp.int32))
        every_key = [a for of in kv for a in of]
        mine = attend(last, lists, pieces, q_two, every_key, state)
        beside = permute(mine, apart(2))
        in_a = permute(mine, across)
        in_b = permute(beside, across)
        out_a = permute(in_a, outward)
        out_b = permute(in_b, outward)
        own, other = project(at, middle, (mine, beside, in_a, in_b, out_a, out_b), w_own, w_swap)
        return own, swap(other)

    theirs = []
    for i in range(2):
        own, come = chunk(2 * (1 - row) + i)
        term = (own + come.astype(jnp.float32)).astype(jnp.bfloat16)
        theirs.append(permute(term, [(0, 1), (1, 0)], "rows"))
    ours = []
    for i in range(2):
        own, come = chunk(2 * row + i)
        ours.append(own + come.astype(jnp.float32) + theirs[i].astype(jnp.float32))
    return jnp.concatenate(ours, axis=0).astype(jnp.bfloat16)


def solution(mesh):
    tensor, rows = mesh.shape["tensor"], mesh.shape["rows"]

    def splits(queries, keyvals):
        return (
            tensor == 8
            and rows == 2
            and keyvals.shape[1] == 4 * 2 * HEAD_WIDTH
            and queries.shape[0] == BLOCK_TOKENS
            and keyvals.shape[0] == 8 * BLOCK_TOKENS
        )

    def shards(queries, keyvals, attending, block_fill, out_weight):
        form = exchanged_shards if splits(queries, keyvals) else gathered_shards
        return form(queries, keyvals, attending, block_fill, out_weight)

    return jax.shard_map(
        shards,
        mesh=mesh,
        in_specs=(
            P(("groups", "tensor"), "rows"),
            P(("groups", "tensor"), "rows"),
            P(("groups", "tensor"), None),
            P(("groups", "tensor")),
            P("rows", "tensor"),
        ),
        out_specs=P(("groups", "rows"), "tensor"),
        check_vma=False,
    )
```

```python
import functools
import math

import jax
import jax.numpy as jnp
from jax import lax
from jax.experimental import pallas as pl
from jax.experimental.pallas import tpu as pltpu
from jax.sharding import PartitionSpec as P


HEAD_WIDTH = 128
BLOCK_TOKENS = 128
masked_low = -1e30
exp2_scale = math.log2(math.e) / math.sqrt(HEAD_WIDTH)
key_group = 4
meta_rows = 16
share = 16
attend_vmem = 16 << 20
project_vmem = 24 << 20
chunks = ((False, 0, 2), (False, 2, 2), (True, 0, 2), (True, 2, 2))


slab_rows = 512


def head_scores(q_heads, key_heads):
    scores = jnp.einsum("hrd,hkd->hrk", q_heads, key_heads, preferred_element_type=jnp.float32)
    return scores * (1.0 / math.sqrt(HEAD_WIDTH))


def fold_keys(q_heads, key_heads, value_heads, visible):
    head_count = key_heads.shape[0]
    row_count = q_heads.shape[1]
    key_count = key_heads.shape[1]
    slab_size = math.gcd(key_count, slab_rows)
    slab_count = key_count // slab_size
    keys_split = jnp.transpose(
        key_heads.reshape(head_count, slab_count, slab_size, HEAD_WIDTH), (1, 0, 2, 3)
    )
    values_split = jnp.transpose(
        value_heads.reshape(head_count, slab_count, slab_size, HEAD_WIDTH), (1, 0, 2, 3)
    )
    visible_split = visible.reshape(slab_count, slab_size)

    def find_top(current, pieces):
        scores = head_scores(q_heads, pieces[0])
        return (
            jnp.maximum(
                current, jnp.max(jnp.where(pieces[1][None, None, :], scores, masked_low), axis=2)
            ),
            None,
        )

    highest, unused = lax.scan(
        find_top,
        jnp.full((head_count, row_count), masked_low, jnp.float32),
        (keys_split, visible_split),
    )

    def accumulate(current, pieces):
        totals, summed = current
        scores = head_scores(q_heads, pieces[0])
        probs = jnp.where(pieces[2][None, None, :], jnp.exp(scores - highest[..., None]), 0.0)
        totals = totals + jnp.sum(probs, axis=2)
        summed = summed + jnp.einsum(
            "hrk,hkd->hrd",
            probs.astype(jnp.bfloat16),
            pieces[1],
            preferred_element_type=jnp.float32,
        )
        return ((totals, summed), None)

    start_state = (
        jnp.zeros((head_count, row_count), jnp.float32),
        jnp.zeros((head_count, row_count, HEAD_WIDTH), jnp.float32),
    )
    final_state, unused = lax.scan(
        accumulate, start_state, (keys_split, values_split, visible_split)
    )
    return final_state[1] / final_state[0][..., None]


def split_heads(kv_rows):
    key_count = kv_rows.shape[0]
    head_count = kv_rows.shape[1] // (2 * HEAD_WIDTH)
    reshaped_tensor = kv_rows.reshape(key_count, head_count, 2, HEAD_WIDTH)
    return (
        jnp.transpose(reshaped_tensor[:, :, 0, :], (1, 0, 2)),
        jnp.transpose(reshaped_tensor[:, :, 1, :], (1, 0, 2)),
    )


def gathered_shards(queries, keyvals, attending, block_fill, out_weight):
    q_len = queries.shape[0]
    head_count = keyvals.shape[1] // (2 * HEAD_WIDTH)
    query_group_width = queries.shape[1] // (HEAD_WIDTH * head_count)
    row_count = q_len * query_group_width
    positions = jnp.arange(BLOCK_TOKENS, dtype=jnp.int32)
    token_ok = positions[None, :] < block_fill[:, None]
    q_heads = jnp.transpose(
        queries.reshape(q_len, head_count, query_group_width, HEAD_WIDTH), (1, 0, 2, 3)
    ).reshape(head_count, row_count, HEAD_WIDTH)
    powers = jnp.sum(jnp.power(2, attending), axis=1).astype(jnp.int32)
    visible_bits = jnp.where(token_ok, powers[:, None], 0).reshape(keyvals.shape[0])
    my_bit = jnp.power(2, lax.axis_index("tensor"))
    all_rows, all_bits = (
        lax.all_gather(keyvals, "tensor", axis=0, tiled=True),
        lax.all_gather(visible_bits, "tensor", axis=0, tiled=True),
    )
    visible = all_bits // my_bit % 2 == 1
    key_heads, value_heads = split_heads(all_rows)
    merged = fold_keys(q_heads, key_heads, value_heads, visible)
    attended_output = jnp.transpose(
        merged.reshape(head_count, q_len, query_group_width, HEAD_WIDTH), (1, 0, 2, 3)
    )
    attended_output = attended_output.reshape(
        q_len, head_count * query_group_width * HEAD_WIDTH
    ).astype(jnp.bfloat16)
    terms = jnp.dot(
        lax.all_gather(attended_output, "tensor", axis=0, tiled=True),
        out_weight,
        preferred_element_type=jnp.float32,
    )
    return lax.psum_scatter(terms, "rows", scatter_dimension=0, tiled=True).astype(jnp.bfloat16)


def query_block(i, pos, part):
    if part is None:
        return i
    mine, offset = part
    return 4 * (pos[2] if mine else 1 - pos[2]) + offset + i


def query_slot(i, pos, part):
    block = query_block(i, pos, part)
    return (block // 2) ^ pos[0], (block % 2) ^ pos[1]


def attend_kernel(folded, part, last, heads, tab, pos, *refs):
    q_refs, refs = refs[:2], refs[2:]
    chips = 4 if last else 1
    kv_refs, refs = refs[: 2 * chips], refs[2 * chips :]
    if last:
        early = chips - len(folded)
        acc_in, refs = refs[:early], refs[early:]
        o_ref, kv, q_rows, sems, acc, top = refs
    else:
        acc_out, kv, q_rows, sems = refs
        acc = acc_out.at[0]
    step = pl.program_id(0)
    width = HEAD_WIDTH
    half = kv_refs[0].shape[0]
    block = query_block(step, pos, part)
    lane = lax.broadcasted_iota(jnp.int32, (1, BLOCK_TOKENS), 1)
    rows = heads * BLOCK_TOKENS
    sums = acc.at[pl.ds(0, rows)]
    high = acc.at[pl.ds(rows, 8), pl.ds(0, BLOCK_TOKENS)]

    def fetch(which, place):
        base = place * share
        copies = [
            pltpu.make_async_copy(
                kv_refs[which * 2 + i], kv.at[pl.ds(base + half * i, half)], sems.at[2 * place + i]
            )
            for i in range(2)
        ]
        for copy in copies:
            copy.start()
        for copy in copies:
            copy.wait()

    def group_of(of, place, j):
        base = place * share
        entries = [tab[of, block, j * key_group + p] for p in range(key_group)]
        hidden = [jnp.where(lane < e % 256, 0.0, masked_low) for e in entries]
        values = jnp.concatenate([kv[base + e // 256, :, width:] for e in entries], axis=0)
        values = jnp.concatenate([values, jnp.ones_like(values)], axis=1)
        keys = [kv[base + e // 256, :, :width] for e in entries]
        return keys, hidden, values

    def groups_of(of):
        return (tab[of, block, share] + (key_group - 1)) // key_group

    def exponents(keys, hidden, i):
        pair = jnp.concatenate(keys[i : i + 2], axis=0)
        scores = lax.dot_general(
            q_rows[...], pair, (((1,), (1,)), ((), ())), preferred_element_type=jnp.float32
        )
        return scores * exp2_scale + jnp.concatenate(hidden[i : i + 2], axis=1)

    @pl.when(step == 0)
    def _():
        for place, of in enumerate(folded):
            fetch(of if last else 0, place)

    other_core = query_slot(step, pos, part)[1]
    for which, q_ref in enumerate(q_refs):

        @pl.when(other_core == which)
        def _():
            for h in range(heads):
                q_rows[h * BLOCK_TOKENS : (h + 1) * BLOCK_TOKENS] = q_ref[
                    0, :, h * width : (h + 1) * width
                ]

    if last:
        sums[...] = functools.reduce(jnp.add, [a[0, :rows] for a in acc_in])
        high[...] = functools.reduce(
            jnp.maximum, [a[0, rows:, :BLOCK_TOKENS] for a in acc_in]
        )
    else:
        acc[...] = jnp.zeros(acc.shape, jnp.float32)
        high[...] = jnp.full(high.shape, masked_low, jnp.float32)

    def fold(of, place, j, carry):
        keys, hidden, values = group_of(of, place, j)
        probs = []
        highest = high[...]
        for i in range(0, key_group, 2):
            x = exponents(keys, hidden, i)
            for side in (x[:, :BLOCK_TOKENS], x[:, BLOCK_TOKENS:]):
                highest = jnp.maximum(highest, jnp.max(side.reshape(-1, 8, BLOCK_TOKENS), axis=0))
            probs.append(jnp.exp2(x).astype(jnp.bfloat16))
        high[...] = highest
        sums[...] += jnp.dot(
            jnp.concatenate(probs, axis=1), values, preferred_element_type=jnp.float32
        )
        return carry

    for place, of in enumerate(folded):
        lax.fori_loop(0, groups_of(of), functools.partial(fold, of, place), 0)
    if not last:
        return

    unsafe = (jnp.max(high[...]) > 100.0) | (jnp.min(sums[:, width:]) < 2.0**-80)

    @pl.when(unsafe)
    def _():
        sums[...] = jnp.zeros(sums.shape, jnp.float32)
        top[...] = jnp.full(top.shape, masked_low, jnp.float32)
        for of in range(chips):
            fetch(of, 0)

            def fold_top(j, carry):
                keys, hidden, values = group_of(of, 0, j)
                for i in range(0, key_group, 2):
                    x = exponents(keys, hidden, i)
                    before = top[...]
                    after = jnp.maximum(before, jnp.max(x, axis=1, keepdims=True))
                    fade = jnp.exp2(before - after)
                    top[...] = after
                    probs = jnp.exp2(x - jnp.concatenate([after, after], axis=1))
                    sums[...] = sums[...] * jnp.concatenate([fade, fade], axis=1) + jnp.dot(
                        probs.astype(jnp.bfloat16),
                        values[i * BLOCK_TOKENS : (i + 2) * BLOCK_TOKENS],
                        preferred_element_type=jnp.float32,
                    )
                return carry

            lax.fori_loop(0, groups_of(of), fold_top, 0)
        fetch(folded[0], 0)

    for h in range(heads):
        at = slice(h * BLOCK_TOKENS, (h + 1) * BLOCK_TOKENS)
        o_ref[:, h * width : (h + 1) * width] = (sums[at, :width] / sums[at, width:]).astype(
            o_ref.dtype
        )


def attend(folded, tab, pos, q_two, kv_refs, count, part=None, state=None):
    last = state is not None
    state = state or []
    width = q_two[0].shape[2]
    heads = width // HEAD_WIDTH
    rows = heads * BLOCK_TOKENS
    q_spec = pl.BlockSpec(
        (1, BLOCK_TOKENS, width), lambda i, tab, pos: (query_slot(i, pos, part)[0], 0, 0)
    )
    acc_block = (1, rows + 8, 2 * HEAD_WIDTH)

    def acc_spec(whole):
        if whole:
            return pl.BlockSpec(acc_block, lambda i, tab, pos: (query_block(i, pos, part), 0, 0))
        return pl.BlockSpec(acc_block, lambda i, tab, pos: (i + (part[1] if last else 0), 0, 0))

    scratch = [
        pltpu.VMEM((len(folded) * share, BLOCK_TOKENS, 2 * HEAD_WIDTH), jnp.bfloat16),
        pltpu.VMEM((rows, HEAD_WIDTH), jnp.bfloat16),
        pltpu.SemaphoreType.DMA((2 * len(folded),)),
    ]
    if last:
        out_shape = jax.ShapeDtypeStruct((count * BLOCK_TOKENS, width), jnp.bfloat16)
        out_specs = pl.BlockSpec((BLOCK_TOKENS, width), lambda i, *_: (i, 0))
        scratch += [
            pltpu.VMEM((rows + 8, 2 * HEAD_WIDTH), jnp.float32),
            pltpu.VMEM((rows, HEAD_WIDTH), jnp.float32),
        ]
    else:
        out_shape = jax.ShapeDtypeStruct((count, rows + 8, 2 * HEAD_WIDTH), jnp.float32)
        out_specs = acc_spec(part is None)
    shape = (kv_refs[0].shape[0] // BLOCK_TOKENS, BLOCK_TOKENS, kv_refs[0].shape[1])
    work = count * len(folded) * share // 2 * rows * BLOCK_TOKENS
    return pl.pallas_call(
        functools.partial(attend_kernel, folded, part, last, heads),
        out_shape=out_shape,
        grid_spec=pltpu.PrefetchScalarGridSpec(
            num_scalar_prefetch=2,
            grid=(count,),
            in_specs=[q_spec] * 2
            + [pl.BlockSpec(memory_space=pl.ANY)] * len(kv_refs)
            + [acc_spec(whole) for whole, _ in state],
            out_specs=out_specs,
            scratch_shapes=scratch,
        ),
        compiler_params=pltpu.CompilerParams(vmem_limit_bytes=attend_vmem),
        cost_estimate=pl.CostEstimate(
            flops=work * 4 * HEAD_WIDTH * 4, bytes_accessed=work // 8, transcendentals=work
        ),
        name="attend",
    )(tab, pos, *q_two, *[a.reshape(shape) for a in kv_refs], *[a for _, a in state])


def piece_chip(i, z):
    far = jnp.where(z < 2, 2, 1)
    return z ^ i if i < 2 else far ^ (i % 2)


def project_kernel(pos, near, come, out, w_own, w_swap, *refs):
    own_ref, other_ref, parts, sems = refs
    ends = (pos[0] == 0) | (pos[0] == 3)

    def bring(i, source):
        return pltpu.make_async_copy(source, parts.at[pl.ds(2 * i, 2)], sems.at[i])

    bring(0, near).start()

    @pl.when(ends)
    def _():
        bring(1, out).start()

    @pl.when(jnp.logical_not(ends))
    def _():
        bring(1, come).start()

    for i in range(2):
        bring(i, near).wait()
    depth = near.shape[2]
    tile = 256
    own_rows = pl.ds(pl.multiple_of(pos[1] * depth, depth), depth)
    places = [piece_chip(i, pos[0]) for i in range(4)]

    for at in range(0, own_ref.shape[1], tile):
        columns = slice(at, at + tile)
        for w_ref, w_rows, o_ref in (
            (w_swap, slice(0, depth), other_ref),
            (w_own, own_rows, own_ref),
        ):
            terms = [
                jnp.dot(
                    parts[i],
                    w_ref[places[i], w_rows, columns],
                    preferred_element_type=jnp.float32,
                )
                for i in range(4)
            ]
            o_ref[:, columns] = functools.reduce(jnp.add, terms).astype(o_ref.dtype)


def project(pos, near, come, out, w_own, w_swap):
    rows, depth = near.shape[1:]
    chips, _, columns = w_own.shape
    vmem = pl.BlockSpec(memory_space=pltpu.VMEM)
    return pl.pallas_call(
        project_kernel,
        out_shape=(
            jax.ShapeDtypeStruct((rows, columns), jnp.float32),
            jax.ShapeDtypeStruct((rows, columns), jnp.bfloat16),
        ),
        in_specs=[pl.BlockSpec(memory_space=pltpu.SMEM)]
        + [pl.BlockSpec(memory_space=pl.ANY)] * 3
        + [vmem] * 2,
        out_specs=(vmem, vmem),
        scratch_shapes=[
            pltpu.VMEM((chips, rows, depth), jnp.bfloat16),
            pltpu.SemaphoreType.DMA((2,)),
        ],
        compiler_params=pltpu.CompilerParams(vmem_limit_bytes=project_vmem),
        cost_estimate=pl.CostEstimate(
            flops=2 * rows * chips * depth * 2 * columns,
            bytes_accessed=2 * (8 * depth * columns + 6 * rows * depth + 3 * rows * columns),
            transcendentals=0,
        ),
        name="project",
    )(pos, near, come, out, w_own, w_swap)


def apart(k):
    return [(i, i ^ k) for i in range(8)]


def key_lists(meta, blocks):
    chips = meta.shape[0]
    naming = meta[:, :, : 8 * 4].reshape(chips, share, 4)
    fill = meta[:, :, 8 * 4 : 8 * 5].reshape(chips, share)
    wanted = jnp.arange(blocks, dtype=jnp.int32)[None, :, None, None]
    listed = jnp.any(naming[:, None] == wanted, axis=3)
    ones = listed.astype(jnp.int32)
    place = jnp.arange(share, dtype=jnp.int32)
    before = jnp.sum(jnp.where(place[None, :] < place[:, None], ones[:, :, None, :], 0), axis=3)
    entry = place * 256 + fill
    tab = jnp.sum(
        jnp.where(
            listed[..., None] & (before[..., None] == place),
            entry[:, None, :, None],
            0,
        ),
        axis=2,
    )
    return jnp.concatenate([tab, jnp.sum(ones, axis=2, keepdims=True)], axis=2)


def permute(array, perm, axis="tensor"):
    return lax.ppermute(array, axis, perm)


def exchanged_shards(queries, keyvals, attending, block_fill, out_weight):
    t = lax.axis_index("tensor")
    z, core = t // 2, t % 2
    row = lax.axis_index("rows")
    chips = 4
    q_len = queries.shape[0]
    wide = queries.shape[1] // chips
    depth = wide // 2
    pair = 2 * HEAD_WIDTH

    def swap(array):
        return permute(array, apart(1))

    meta = jnp.concatenate([attending.reshape(-1), block_fill]).astype(jnp.bfloat16)
    meta = jnp.pad(meta[None, :], ((0, meta_rows - 1), (0, depth - meta.shape[0])))
    meta = jnp.concatenate([meta, meta], axis=1)

    def q_for(chip):
        own = lax.dynamic_slice(queries, (0, chip * wide), (q_len, wide))
        return jnp.concatenate([own, meta], axis=0)

    def kv_for(chip):
        return lax.dynamic_slice(keyvals, (0, chip * pair), (keyvals.shape[0], pair))

    def columns_of(arrays, which):
        size = (q_len + meta_rows, depth)
        return jnp.stack([lax.dynamic_slice(a, (0, which * depth), size) for a in arrays])

    q_come = [q_for(z)]
    for k in range(1, chips):
        q_come.append(permute(q_for(z ^ k), apart(2 * k)))
    kv = []
    for k in range(chips):
        own = kv_for(z ^ k)
        if k:
            own = permute(own, apart(2 * k))
        kv.append((own, swap(own)))

    q_own = columns_of(q_come, core)
    q_swap = swap(columns_of(q_come, 1 - core))
    q_two = (q_own, q_swap)
    notes = jnp.stack([q_own[:, q_len, :64], q_swap[:, q_len, :64]], axis=1)
    tab = key_lists(notes.astype(jnp.int32), 2 * chips)
    pos = jnp.stack([z, core, row]).astype(jnp.int32)
    q_two = (q_own, q_swap)
    whole = [attend((k,), tab, pos, q_two, kv[k], 2 * chips) for k in range(2)]
    halves = [attend((2,), tab, pos, q_two, kv[2], chips, (mine, 0)) for mine in (False, True)]

    w_own = out_weight.reshape(chips, wide, out_weight.shape[1])
    w_swap = lax.dynamic_slice(
        w_own, (0, (1 - core) * depth, 0), (chips, depth, out_weight.shape[1])
    )
    w_swap = swap(w_swap)
    across = [(2, 4), (3, 5), (4, 2), (5, 3)]
    outward = [(2, 0), (3, 1), (4, 6), (5, 7)]
    every_key = [a for of in kv for a in of]

    def chunk(part, count):
        state = [(True, a) for a in whole] + [(False, halves[part[0]])]
        mine = attend((3,), tab, pos, q_two, every_key, count, part, state)
        near = jnp.stack([mine, permute(mine, apart(2))])
        come = permute(near, across)
        out = permute(come, outward)
        own, other = project(pos, near, come, out, w_own, w_swap)
        return own, swap(other)

    theirs = []
    ours = []
    for mine, offset, count in chunks:
        own, come = chunk((mine, offset), count)
        total = own + come.astype(jnp.float32)
        if mine:
            come = jnp.concatenate(theirs, axis=0) if len(theirs) > 1 else theirs[0]
            come = come[offset * BLOCK_TOKENS : (offset + count) * BLOCK_TOKENS]
            ours.append((total + come.astype(jnp.float32)).astype(jnp.bfloat16))
        else:
            sent = total.astype(jnp.bfloat16)
            theirs.append(permute(sent, [(0, 1), (1, 0)], "rows"))
    return jnp.concatenate(ours, axis=0)


def solution(mesh):
    tensor, rows = mesh.shape["tensor"], mesh.shape["rows"]

    def splits(queries, keyvals):
        return (
            tensor == 8
            and rows == 2
            and keyvals.shape[1] == 4 * 2 * HEAD_WIDTH
            and queries.shape[0] == BLOCK_TOKENS
            and keyvals.shape[0] == 8 * BLOCK_TOKENS
        )

    def shards(queries, keyvals, attending, block_fill, out_weight):
        form = exchanged_shards if splits(queries, keyvals) else gathered_shards
        return form(queries, keyvals, attending, block_fill, out_weight)

    return jax.shard_map(
        shards,
        mesh=mesh,
        in_specs=(
            P(("groups", "tensor"), "rows"),
            P(("groups", "tensor"), "rows"),
            P(("groups", "tensor"), None),
            P(("groups", "tensor")),
            P("rows", "tensor"),
        ),
        out_specs=P(("groups", "rows"), "tensor"),
        check_vma=False,
    )
```

```python
import functools
import math

import jax
import jax.numpy as jnp
from jax import lax
from jax.experimental import pallas as pl
from jax.experimental.pallas import tpu as pltpu
from jax.sharding import PartitionSpec as P


HEAD_WIDTH = 128
BLOCK_TOKENS = 128
masked_low = -1e30
exp2_scale = math.log2(math.e) / math.sqrt(HEAD_WIDTH)
key_group = 4
meta_rows = 16
share = 16
attend_vmem = 16 << 20
project_vmem = 24 << 20
chunks = ((False, 0, 2), (False, 2, 2), (True, 0, 2), (True, 2, 2))


slab_rows = 512


def head_scores(q_heads, key_heads):
    scores = jnp.einsum("hrd,hkd->hrk", q_heads, key_heads, preferred_element_type=jnp.float32)
    return scores * (1.0 / math.sqrt(HEAD_WIDTH))


def fold_keys(q_heads, key_heads, value_heads, visible):
    head_count = key_heads.shape[0]
    row_count = q_heads.shape[1]
    key_count = key_heads.shape[1]
    slab_size = math.gcd(key_count, slab_rows)
    slab_count = key_count // slab_size
    keys_split = jnp.transpose(
        key_heads.reshape(head_count, slab_count, slab_size, HEAD_WIDTH), (1, 0, 2, 3)
    )
    values_split = jnp.transpose(
        value_heads.reshape(head_count, slab_count, slab_size, HEAD_WIDTH), (1, 0, 2, 3)
    )
    visible_split = visible.reshape(slab_count, slab_size)

    def find_top(current, pieces):
        scores = head_scores(q_heads, pieces[0])
        return (
            jnp.maximum(
                current, jnp.max(jnp.where(pieces[1][None, None, :], scores, masked_low), axis=2)
            ),
            None,
        )

    highest, unused = lax.scan(
        find_top,
        jnp.full((head_count, row_count), masked_low, jnp.float32),
        (keys_split, visible_split),
    )

    def accumulate(current, pieces):
        totals, summed = current
        scores = head_scores(q_heads, pieces[0])
        probs = jnp.where(pieces[2][None, None, :], jnp.exp(scores - highest[..., None]), 0.0)
        totals = totals + jnp.sum(probs, axis=2)
        summed = summed + jnp.einsum(
            "hrk,hkd->hrd",
            probs.astype(jnp.bfloat16),
            pieces[1],
            preferred_element_type=jnp.float32,
        )
        return ((totals, summed), None)

    start_state = (
        jnp.zeros((head_count, row_count), jnp.float32),
        jnp.zeros((head_count, row_count, HEAD_WIDTH), jnp.float32),
    )
    final_state, unused = lax.scan(
        accumulate, start_state, (keys_split, values_split, visible_split)
    )
    return final_state[1] / final_state[0][..., None]


def split_heads(kv_rows):
    key_count = kv_rows.shape[0]
    head_count = kv_rows.shape[1] // (2 * HEAD_WIDTH)
    reshaped_tensor = kv_rows.reshape(key_count, head_count, 2, HEAD_WIDTH)
    return (
        jnp.transpose(reshaped_tensor[:, :, 0, :], (1, 0, 2)),
        jnp.transpose(reshaped_tensor[:, :, 1, :], (1, 0, 2)),
    )


def gathered_shards(queries, keyvals, attending, block_fill, out_weight):
    q_len = queries.shape[0]
    head_count = keyvals.shape[1] // (2 * HEAD_WIDTH)
    query_group_width = queries.shape[1] // (HEAD_WIDTH * head_count)
    row_count = q_len * query_group_width
    positions = jnp.arange(BLOCK_TOKENS, dtype=jnp.int32)
    token_ok = positions[None, :] < block_fill[:, None]
    q_heads = jnp.transpose(
        queries.reshape(q_len, head_count, query_group_width, HEAD_WIDTH), (1, 0, 2, 3)
    ).reshape(head_count, row_count, HEAD_WIDTH)
    powers = jnp.sum(jnp.power(2, attending), axis=1).astype(jnp.int32)
    visible_bits = jnp.where(token_ok, powers[:, None], 0).reshape(keyvals.shape[0])
    my_bit = jnp.power(2, lax.axis_index("tensor"))
    all_rows, all_bits = (
        lax.all_gather(keyvals, "tensor", axis=0, tiled=True),
        lax.all_gather(visible_bits, "tensor", axis=0, tiled=True),
    )
    visible = all_bits // my_bit % 2 == 1
    key_heads, value_heads = split_heads(all_rows)
    merged = fold_keys(q_heads, key_heads, value_heads, visible)
    attended_output = jnp.transpose(
        merged.reshape(head_count, q_len, query_group_width, HEAD_WIDTH), (1, 0, 2, 3)
    )
    attended_output = attended_output.reshape(
        q_len, head_count * query_group_width * HEAD_WIDTH
    ).astype(jnp.bfloat16)
    terms = jnp.dot(
        lax.all_gather(attended_output, "tensor", axis=0, tiled=True),
        out_weight,
        preferred_element_type=jnp.float32,
    )
    return lax.psum_scatter(terms, "rows", scatter_dimension=0, tiled=True).astype(jnp.bfloat16)


def query_block(i, pos, part):
    if part is None:
        return i
    mine, offset = part
    return 4 * (pos[2] if mine else 1 - pos[2]) + offset + i


def query_slot(i, pos, part):
    block = query_block(i, pos, part)
    return (block // 2) ^ pos[0], (block % 2) ^ pos[1]


def attend_kernel(folded, part, last, heads, tab, pos, *refs):
    q_refs, refs = refs[:2], refs[2:]
    chips = 4 if last else 1
    kv_refs, refs = refs[: 2 * chips], refs[2 * chips :]
    if last:
        early = chips - len(folded)
        acc_in, refs = refs[:early], refs[early:]
        o_ref, kv, q_rows, sems, acc, top = refs
    else:
        acc_out, kv, q_rows, sems = refs
        acc = acc_out.at[0]
    step = pl.program_id(0)
    width = HEAD_WIDTH
    half = kv_refs[0].shape[0]
    block = query_block(step, pos, part)
    lane = lax.broadcasted_iota(jnp.int32, (1, BLOCK_TOKENS), 1)
    rows = heads * BLOCK_TOKENS
    sums = acc.at[pl.ds(0, rows)]
    high = acc.at[pl.ds(rows, 8), pl.ds(0, BLOCK_TOKENS)]

    def fetch(which, place):
        base = place * share
        copies = [
            pltpu.make_async_copy(
                kv_refs[which * 2 + i], kv.at[pl.ds(base + half * i, half)], sems.at[2 * place + i]
            )
            for i in range(2)
        ]
        for copy in copies:
            copy.start()
        for copy in copies:
            copy.wait()

    def group_of(of, place, j):
        base = place * share
        entries = [tab[of, block, j * key_group + p] for p in range(key_group)]
        hidden = [jnp.where(lane < e % 256, 0.0, masked_low) for e in entries]
        values = jnp.concatenate([kv[base + e // 256, :, width:] for e in entries], axis=0)
        values = jnp.concatenate([values, jnp.ones_like(values)], axis=1)
        keys = [kv[base + e // 256, :, :width] for e in entries]
        return keys, hidden, values

    def groups_of(of):
        return (tab[of, block, share] + (key_group - 1)) // key_group

    def exponents(keys, hidden, i, some=slice(None)):
        pair = jnp.concatenate(keys[i : i + 2], axis=0)
        scores = lax.dot_general(
            q_rows[some], pair, (((1,), (1,)), ((), ())), preferred_element_type=jnp.float32
        )
        return scores * exp2_scale + jnp.concatenate(hidden[i : i + 2], axis=1)

    @pl.when(step == 0)
    def _():
        for place, of in enumerate(folded):
            fetch(of if last else 0, place)

    other_core = query_slot(step, pos, part)[1]
    for which, q_ref in enumerate(q_refs):

        @pl.when(other_core == which)
        def _():
            for h in range(heads):
                q_rows[h * BLOCK_TOKENS : (h + 1) * BLOCK_TOKENS] = q_ref[
                    0, :, h * width : (h + 1) * width
                ]

    if last:
        sums[...] = functools.reduce(jnp.add, [a[0, :rows] for a in acc_in])
        high[...] = functools.reduce(
            jnp.maximum, [a[0, rows:, :BLOCK_TOKENS] for a in acc_in]
        )
    else:
        acc[...] = jnp.zeros(acc.shape, jnp.float32)
        high[...] = jnp.full(high.shape, masked_low, jnp.float32)

    def fold(of, place, j, carry):
        keys, hidden, values = group_of(of, place, j)
        highest = high[...]
        for at in range(0, rows, rows // 2):
            some = slice(at, at + rows // 2)
            probs = []
            for i in range(0, key_group, 2):
                x = exponents(keys, hidden, i, some)
                for side in (x[:, :BLOCK_TOKENS], x[:, BLOCK_TOKENS:]):
                    side = jnp.max(side.reshape(-1, 8, BLOCK_TOKENS), axis=0)
                    highest = jnp.maximum(highest, side)
                probs.append(jnp.exp2(x).astype(jnp.bfloat16))
            probs = jnp.concatenate(probs, axis=1)
            sums[some] += jnp.dot(probs, values, preferred_element_type=jnp.float32)
        high[...] = highest
        return carry

    for place, of in enumerate(folded):
        lax.fori_loop(0, groups_of(of), functools.partial(fold, of, place), 0)
    if not last:
        return

    unsafe = (jnp.max(high[...]) > 100.0) | (jnp.min(sums[:, width:]) < 2.0**-80)

    @pl.when(unsafe)
    def _():
        sums[...] = jnp.zeros(sums.shape, jnp.float32)
        top[...] = jnp.full(top.shape, masked_low, jnp.float32)
        for of in range(chips):
            fetch(of, 0)

            def fold_top(j, carry):
                keys, hidden, values = group_of(of, 0, j)
                for i in range(0, key_group, 2):
                    x = exponents(keys, hidden, i)
                    before = top[...]
                    after = jnp.maximum(before, jnp.max(x, axis=1, keepdims=True))
                    fade = jnp.exp2(before - after)
                    top[...] = after
                    probs = jnp.exp2(x - jnp.concatenate([after, after], axis=1))
                    sums[...] = sums[...] * jnp.concatenate([fade, fade], axis=1) + jnp.dot(
                        probs.astype(jnp.bfloat16),
                        values[i * BLOCK_TOKENS : (i + 2) * BLOCK_TOKENS],
                        preferred_element_type=jnp.float32,
                    )
                return carry

            lax.fori_loop(0, groups_of(of), fold_top, 0)
        fetch(folded[0], 0)

    for h in range(heads):
        at = slice(h * BLOCK_TOKENS, (h + 1) * BLOCK_TOKENS)
        o_ref[:, h * width : (h + 1) * width] = (sums[at, :width] / sums[at, width:]).astype(
            o_ref.dtype
        )


def attend(folded, tab, pos, q_two, kv_refs, count, part=None, state=None):
    last = state is not None
    state = state or []
    width = q_two[0].shape[2]
    heads = width // HEAD_WIDTH
    rows = heads * BLOCK_TOKENS
    q_spec = pl.BlockSpec(
        (1, BLOCK_TOKENS, width), lambda i, tab, pos: (query_slot(i, pos, part)[0], 0, 0)
    )
    acc_block = (1, rows + 8, 2 * HEAD_WIDTH)

    def acc_spec(whole):
        if whole:
            return pl.BlockSpec(acc_block, lambda i, tab, pos: (query_block(i, pos, part), 0, 0))
        return pl.BlockSpec(acc_block, lambda i, tab, pos: (i + (part[1] if last else 0), 0, 0))

    scratch = [
        pltpu.VMEM((len(folded) * share, BLOCK_TOKENS, 2 * HEAD_WIDTH), jnp.bfloat16),
        pltpu.VMEM((rows, HEAD_WIDTH), jnp.bfloat16),
        pltpu.SemaphoreType.DMA((2 * len(folded),)),
    ]
    if last:
        out_shape = jax.ShapeDtypeStruct((count * BLOCK_TOKENS, width), jnp.bfloat16)
        out_specs = pl.BlockSpec((BLOCK_TOKENS, width), lambda i, *_: (i, 0))
        scratch += [
            pltpu.VMEM((rows + 8, 2 * HEAD_WIDTH), jnp.float32),
            pltpu.VMEM((rows, HEAD_WIDTH), jnp.float32),
        ]
    else:
        out_shape = jax.ShapeDtypeStruct((count, rows + 8, 2 * HEAD_WIDTH), jnp.float32)
        out_specs = acc_spec(part is None)
    shape = (kv_refs[0].shape[0] // BLOCK_TOKENS, BLOCK_TOKENS, kv_refs[0].shape[1])
    work = count * len(folded) * share // 2 * rows * BLOCK_TOKENS
    return pl.pallas_call(
        functools.partial(attend_kernel, folded, part, last, heads),
        out_shape=out_shape,
        grid_spec=pltpu.PrefetchScalarGridSpec(
            num_scalar_prefetch=2,
            grid=(count,),
            in_specs=[q_spec] * 2
            + [pl.BlockSpec(memory_space=pl.ANY)] * len(kv_refs)
            + [acc_spec(whole) for whole, _ in state],
            out_specs=out_specs,
            scratch_shapes=scratch,
        ),
        compiler_params=pltpu.CompilerParams(vmem_limit_bytes=attend_vmem),
        cost_estimate=pl.CostEstimate(
            flops=work * 4 * HEAD_WIDTH * 4, bytes_accessed=work // 8, transcendentals=work
        ),
        name="attend",
    )(tab, pos, *q_two, *[a.reshape(shape) for a in kv_refs], *[a for _, a in state])


def piece_chip(i, z):
    far = jnp.where(z < 2, 2, 1)
    return z ^ i if i < 2 else far ^ (i % 2)


def project_kernel(sides, held, far, pos, near, *refs):
    come, out = refs[:2] if far else (near, near)
    refs = refs[2 * far :]
    w_refs, refs = refs[:sides], refs[sides:]
    bases, refs = refs[: sides * held], refs[sides * held :]
    o_refs, (parts, sems) = refs[:sides], refs[sides:]
    ends = (pos[0] == 0) | (pos[0] == 3)

    def bring(i, source):
        return pltpu.make_async_copy(source, parts.at[pl.ds(2 * i, 2)], sems.at[i])

    if not held:
        bring(0, near).start()
    if far:

        @pl.when(ends)
        def _():
            bring(1, out).start()

        @pl.when(jnp.logical_not(ends))
        def _():
            bring(1, come).start()

    used = range(2 * held, 4 if far else 2)
    for i in range(used.start // 2, used.stop // 2):
        bring(i, near).wait()
    depth = near.shape[2]
    tile = 256
    own_rows = pl.ds(pl.multiple_of(pos[1] * depth, depth), depth)
    places = [piece_chip(i, pos[0]) for i in range(4)]

    for at in range(0, o_refs[0].shape[1], tile):
        columns = slice(at, at + tile)
        for side, (w_ref, o_ref) in enumerate(zip(w_refs, o_refs)):
            w_rows = own_rows if w_ref.shape[1] > depth else slice(0, depth)
            terms = [
                jnp.dot(
                    parts[i],
                    w_ref[places[i], w_rows, columns],
                    preferred_element_type=jnp.float32,
                )
                for i in used
            ]
            if held:
                terms.append(bases[side][:, columns])
            o_ref[:, columns] = functools.reduce(jnp.add, terms).astype(o_ref.dtype)


def project(pos, near, far, weights, types, bases=()):
    rows, depth = near.shape[1:]
    chips, _, columns = weights[0].shape
    sides = len(weights)
    vmem = pl.BlockSpec(memory_space=pltpu.VMEM)
    return pl.pallas_call(
        functools.partial(project_kernel, sides, bool(bases), bool(far)),
        out_shape=tuple(jax.ShapeDtypeStruct((rows, columns), kind) for kind in types),
        in_specs=[pl.BlockSpec(memory_space=pltpu.SMEM)]
        + [pl.BlockSpec(memory_space=pl.ANY)] * (1 + len(far))
        + [vmem] * (sides + len(bases)),
        out_specs=(vmem,) * sides,
        scratch_shapes=[
            pltpu.VMEM((chips, rows, depth), jnp.bfloat16),
            pltpu.SemaphoreType.DMA((2,)),
        ],
        compiler_params=pltpu.CompilerParams(vmem_limit_bytes=project_vmem),
        cost_estimate=pl.CostEstimate(
            flops=2 * rows * chips * depth * sides * columns,
            bytes_accessed=2 * sides * (chips * depth + 3 * rows) * columns,
            transcendentals=0,
        ),
        name="project",
    )(pos, near, *far, *weights, *bases)


def finish_kernel(own, come, theirs, *refs):
    total = own[...] + come[...].astype(jnp.float32) + theirs[...].astype(jnp.float32)
    refs[-1][...] = total.astype(jnp.bfloat16)


def finish(at, size, own, come, theirs, result=None):
    rows, columns = own.shape
    block = pl.BlockSpec((rows, columns), lambda i: (0, 0))
    held = () if result is None else (result,)
    return pl.pallas_call(
        finish_kernel,
        out_shape=jax.ShapeDtypeStruct((size, columns), jnp.bfloat16),
        grid=(1,),
        in_specs=[block] * 3 + [pl.BlockSpec(memory_space=pl.ANY)] * len(held),
        out_specs=pl.BlockSpec((rows, columns), lambda i: (at, 0)),
        input_output_aliases={3: 0} if held else {},
        compiler_params=pltpu.CompilerParams(vmem_limit_bytes=attend_vmem),
        name="finish",
    )(own, come, theirs, *held)


def apart(k):
    return [(i, i ^ k) for i in range(8)]


def key_lists(meta, blocks):
    chips = meta.shape[0]
    naming = meta[:, :, : 8 * 4].reshape(chips, share, 4)
    fill = meta[:, :, 8 * 4 : 8 * 5].reshape(chips, share)
    wanted = jnp.arange(blocks, dtype=jnp.int32)[None, :, None, None]
    listed = jnp.any(naming[:, None] == wanted, axis=3)
    ones = listed.astype(jnp.int32)
    place = jnp.arange(share, dtype=jnp.int32)
    before = jnp.sum(jnp.where(place[None, :] < place[:, None], ones[:, :, None, :], 0), axis=3)
    entry = place * 256 + fill
    tab = jnp.sum(
        jnp.where(
            listed[..., None] & (before[..., None] == place),
            entry[:, None, :, None],
            0,
        ),
        axis=2,
    )
    return jnp.concatenate([tab, jnp.sum(ones, axis=2, keepdims=True)], axis=2)


def permute(array, perm, axis="tensor"):
    return lax.ppermute(array, axis, perm)


def exchanged_shards(queries, keyvals, attending, block_fill, out_weight):
    t = lax.axis_index("tensor")
    z, core = t // 2, t % 2
    row = lax.axis_index("rows")
    chips = 4
    q_len = queries.shape[0]
    wide = queries.shape[1] // chips
    depth = wide // 2
    pair = 2 * HEAD_WIDTH

    def swap(array):
        return permute(array, apart(1))

    def q_for(chip):
        return lax.dynamic_slice(queries, (0, chip * wide), (q_len, wide))

    def kv_for(chip):
        return lax.dynamic_slice(keyvals, (0, chip * pair), (keyvals.shape[0], pair))

    def columns_of(arrays, which):
        size = (q_len, depth)
        return jnp.stack([lax.dynamic_slice(a, (0, which * depth), size) for a in arrays])

    q_come = [q_for(z)]
    for k in range(1, chips):
        q_come.append(permute(q_for(z ^ k), apart(2 * k)))
    note = jnp.concatenate([attending.reshape(-1), block_fill]).astype(jnp.bfloat16)
    note = jnp.pad(note[None, :], ((0, meta_rows - 1), (0, HEAD_WIDTH - note.shape[0])))
    notes = [note] + [permute(note, apart(2 * k)) for k in range(1, chips)]
    kv = []
    for k in range(chips):
        own = kv_for(z ^ k)
        if k:
            own = permute(own, apart(2 * k))
        kv.append((own, swap(own)))

    q_own = columns_of(q_come, core)
    q_swap = swap(columns_of(q_come, 1 - core))
    q_two = (q_own, q_swap)
    notes = jnp.stack(notes)
    notes = jnp.stack([notes[:, 0, :64], swap(notes)[:, 0, :64]], axis=1)
    tab = key_lists(notes.astype(jnp.int32), 2 * chips)
    pos = jnp.stack([z, core, row]).astype(jnp.int32)
    q_two = (q_own, q_swap)
    whole = [attend((k,), tab, pos, q_two, kv[k], 2 * chips) for k in range(2)]
    halves = [attend((2,), tab, pos, q_two, kv[2], chips, (mine, 0)) for mine in (False, True)]

    w_own = out_weight.reshape(chips, wide, out_weight.shape[1])
    w_swap = lax.dynamic_slice(
        w_own, (0, (1 - core) * depth, 0), (chips, depth, out_weight.shape[1])
    )
    w_swap = swap(w_swap)
    across = [(2, 4), (3, 5), (4, 2), (5, 3)]
    outward = [(2, 0), (3, 1), (4, 6), (5, 7)]
    every_key = [a for of in kv for a in of]

    def chunk(i, part, count):
        state = [(True, a) for a in whole] + [(False, halves[part[0]])]
        mine = attend((3,), tab, pos, q_two, every_key, count, part, state)
        near = jnp.stack([mine, permute(mine, apart(2))])
        come = permute(near, across)
        out = permute(come, outward)
        far = (come, out)
        if i + 1 < len(chunks):
            both = (w_swap, w_own), (jnp.bfloat16, jnp.float32)
            other, own = project(pos, near, far, *both)
        else:
            both = (w_swap, w_own), (jnp.float32, jnp.float32)
            bases = project(pos, near, (), *both)
            (other,) = project(pos, near, far, (w_swap,), (jnp.bfloat16,), bases[:1])
            (own,) = project(pos, near, far, (w_own,), (jnp.float32,), bases[1:])
        return own, swap(other)

    theirs = []
    result = None
    for i, (mine, offset, count) in enumerate(chunks):
        own, come = chunk(i, (mine, offset), count)
        if mine:
            other = theirs[offset // count]
            result = finish(offset // count, q_len * 4, own, come, other, result)
        else:
            sent = (own + come.astype(jnp.float32)).astype(jnp.bfloat16)
            theirs.append(permute(sent, [(0, 1), (1, 0)], "rows"))
    return result


def solution(mesh):
    tensor, rows = mesh.shape["tensor"], mesh.shape["rows"]

    def splits(queries, keyvals):
        return (
            tensor == 8
            and rows == 2
            and keyvals.shape[1] == 4 * 2 * HEAD_WIDTH
            and queries.shape[0] == BLOCK_TOKENS
            and keyvals.shape[0] == 8 * BLOCK_TOKENS
        )

    def shards(queries, keyvals, attending, block_fill, out_weight):
        form = exchanged_shards if splits(queries, keyvals) else gathered_shards
        return form(queries, keyvals, attending, block_fill, out_weight)

    return jax.shard_map(
        shards,
        mesh=mesh,
        in_specs=(
            P(("groups", "tensor"), "rows"),
            P(("groups", "tensor"), "rows"),
            P(("groups", "tensor"), None),
            P(("groups", "tensor")),
            P("rows", "tensor"),
        ),
        out_specs=P(("groups", "rows"), "tensor"),
        check_vma=False,
    )
```

```python
import functools
import math

import jax
import jax.numpy as jnp
from jax import lax
from jax.experimental import pallas as pl
from jax.experimental.pallas import tpu as pltpu
from jax.sharding import PartitionSpec as P


HEAD_WIDTH = 128
BLOCK_TOKENS = 128
masked_low = -1e30
exp2_scale = math.log2(math.e) / math.sqrt(HEAD_WIDTH)
key_group = 4
meta_rows = 16
share = 16
attend_vmem = 16 << 20
project_vmem = 24 << 20
chunks = ((False, 0, 2), (False, 2, 2), (True, 0, 2), (True, 2, 2))


slab_rows = 512


def head_scores(q_heads, key_heads):
    scores = jnp.einsum("hrd,hkd->hrk", q_heads, key_heads, preferred_element_type=jnp.float32)
    return scores * (1.0 / math.sqrt(HEAD_WIDTH))


def fold_keys(q_heads, key_heads, value_heads, visible):
    head_count = key_heads.shape[0]
    row_count = q_heads.shape[1]
    key_count = key_heads.shape[1]
    slab_size = math.gcd(key_count, slab_rows)
    slab_count = key_count // slab_size
    keys_split = jnp.transpose(
        key_heads.reshape(head_count, slab_count, slab_size, HEAD_WIDTH), (1, 0, 2, 3)
    )
    values_split = jnp.transpose(
        value_heads.reshape(head_count, slab_count, slab_size, HEAD_WIDTH), (1, 0, 2, 3)
    )
    visible_split = visible.reshape(slab_count, slab_size)

    def find_top(current, pieces):
        scores = head_scores(q_heads, pieces[0])
        return (
            jnp.maximum(
                current, jnp.max(jnp.where(pieces[1][None, None, :], scores, masked_low), axis=2)
            ),
            None,
        )

    highest, unused = lax.scan(
        find_top,
        jnp.full((head_count, row_count), masked_low, jnp.float32),
        (keys_split, visible_split),
    )

    def accumulate(current, pieces):
        totals, summed = current
        scores = head_scores(q_heads, pieces[0])
        probs = jnp.where(pieces[2][None, None, :], jnp.exp(scores - highest[..., None]), 0.0)
        totals = totals + jnp.sum(probs, axis=2)
        summed = summed + jnp.einsum(
            "hrk,hkd->hrd",
            probs.astype(jnp.bfloat16),
            pieces[1],
            preferred_element_type=jnp.float32,
        )
        return ((totals, summed), None)

    start_state = (
        jnp.zeros((head_count, row_count), jnp.float32),
        jnp.zeros((head_count, row_count, HEAD_WIDTH), jnp.float32),
    )
    final_state, unused = lax.scan(
        accumulate, start_state, (keys_split, values_split, visible_split)
    )
    return final_state[1] / final_state[0][..., None]


def split_heads(kv_rows):
    key_count = kv_rows.shape[0]
    head_count = kv_rows.shape[1] // (2 * HEAD_WIDTH)
    reshaped_tensor = kv_rows.reshape(key_count, head_count, 2, HEAD_WIDTH)
    return (
        jnp.transpose(reshaped_tensor[:, :, 0, :], (1, 0, 2)),
        jnp.transpose(reshaped_tensor[:, :, 1, :], (1, 0, 2)),
    )


def gathered_shards(queries, keyvals, attending, block_fill, out_weight):
    q_len = queries.shape[0]
    head_count = keyvals.shape[1] // (2 * HEAD_WIDTH)
    query_group_width = queries.shape[1] // (HEAD_WIDTH * head_count)
    row_count = q_len * query_group_width
    positions = jnp.arange(BLOCK_TOKENS, dtype=jnp.int32)
    token_ok = positions[None, :] < block_fill[:, None]
    q_heads = jnp.transpose(
        queries.reshape(q_len, head_count, query_group_width, HEAD_WIDTH), (1, 0, 2, 3)
    ).reshape(head_count, row_count, HEAD_WIDTH)
    powers = jnp.sum(jnp.power(2, attending), axis=1).astype(jnp.int32)
    visible_bits = jnp.where(token_ok, powers[:, None], 0).reshape(keyvals.shape[0])
    my_bit = jnp.power(2, lax.axis_index("tensor"))
    all_rows, all_bits = (
        lax.all_gather(keyvals, "tensor", axis=0, tiled=True),
        lax.all_gather(visible_bits, "tensor", axis=0, tiled=True),
    )
    visible = all_bits // my_bit % 2 == 1
    key_heads, value_heads = split_heads(all_rows)
    merged = fold_keys(q_heads, key_heads, value_heads, visible)
    attended_output = jnp.transpose(
        merged.reshape(head_count, q_len, query_group_width, HEAD_WIDTH), (1, 0, 2, 3)
    )
    attended_output = attended_output.reshape(
        q_len, head_count * query_group_width * HEAD_WIDTH
    ).astype(jnp.bfloat16)
    terms = jnp.dot(
        lax.all_gather(attended_output, "tensor", axis=0, tiled=True),
        out_weight,
        preferred_element_type=jnp.float32,
    )
    return lax.psum_scatter(terms, "rows", scatter_dimension=0, tiled=True).astype(jnp.bfloat16)


def query_block(i, pos, part):
    if part is None:
        return i
    mine, offset = part
    return 4 * (pos[2] if mine else 1 - pos[2]) + offset + i


def query_slot(i, pos, part):
    block = query_block(i, pos, part)
    return (block // 2) ^ pos[0], (block % 2) ^ pos[1]


def attend_kernel(folded, part, last, heads, tab, pos, *refs):
    q_refs, refs = refs[:2], refs[2:]
    chips = 4 if last else 1
    kv_refs, refs = refs[: 2 * chips], refs[2 * chips :]
    if last:
        early = chips - len(folded)
        acc_in, refs = refs[:early], refs[early:]
        o_ref, kv, q_rows, sems, acc, top = refs
    else:
        acc_out, kv, q_rows, sems = refs
        acc = acc_out.at[0]
    step = pl.program_id(0)
    width = HEAD_WIDTH
    half = kv_refs[0].shape[0]
    block = query_block(step, pos, part)
    lane = lax.broadcasted_iota(jnp.int32, (1, BLOCK_TOKENS), 1)
    rows = heads * BLOCK_TOKENS
    sums = acc.at[pl.ds(0, rows)]
    high = acc.at[pl.ds(rows, 8), pl.ds(0, BLOCK_TOKENS)]

    def fetch(which, place):
        base = place * share
        copies = [
            pltpu.make_async_copy(
                kv_refs[which * 2 + i], kv.at[pl.ds(base + half * i, half)], sems.at[2 * place + i]
            )
            for i in range(2)
        ]
        for copy in copies:
            copy.start()
        for copy in copies:
            copy.wait()

    def group_of(of, place, j):
        base = place * share
        entries = [tab[of, block, j * key_group + p] for p in range(key_group)]
        hidden = [jnp.where(lane < e % 256, 0.0, masked_low) for e in entries]
        values = jnp.concatenate([kv[base + e // 256, :, width:] for e in entries], axis=0)
        values = jnp.concatenate([values, jnp.ones_like(values)], axis=1)
        keys = [kv[base + e // 256, :, :width] for e in entries]
        return keys, hidden, values

    def groups_of(of):
        return (tab[of, block, share] + (key_group - 1)) // key_group

    def exponents(keys, hidden, i, some=slice(None)):
        pair = jnp.concatenate(keys[i : i + 2], axis=0)
        scores = lax.dot_general(
            q_rows[some], pair, (((1,), (1,)), ((), ())), preferred_element_type=jnp.float32
        )
        return scores * exp2_scale + jnp.concatenate(hidden[i : i + 2], axis=1)

    @pl.when(step == 0)
    def _():
        for place, of in enumerate(folded):
            fetch(of if last else 0, place)

    other_core = query_slot(step, pos, part)[1]
    for which, q_ref in enumerate(q_refs):

        @pl.when(other_core == which)
        def _():
            for h in range(heads):
                q_rows[h * BLOCK_TOKENS : (h + 1) * BLOCK_TOKENS] = q_ref[
                    0, :, h * width : (h + 1) * width
                ]

    if last:
        sums[...] = functools.reduce(jnp.add, [a[0, :rows] for a in acc_in])
        high[...] = functools.reduce(
            jnp.maximum, [a[0, rows:, :BLOCK_TOKENS] for a in acc_in]
        )
    else:
        acc[...] = jnp.zeros(acc.shape, jnp.float32)
        high[...] = jnp.full(high.shape, masked_low, jnp.float32)

    def fold(of, place, j, carry):
        keys, hidden, values = group_of(of, place, j)
        highest = high[...]
        for at in range(0, rows, rows // 2):
            some = slice(at, at + rows // 2)
            probs = []
            for i in range(0, key_group, 2):
                x = exponents(keys, hidden, i, some)
                for side in (x[:, :BLOCK_TOKENS], x[:, BLOCK_TOKENS:]):
                    side = jnp.max(side.reshape(-1, 8, BLOCK_TOKENS), axis=0)
                    highest = jnp.maximum(highest, side)
                probs.append(jnp.exp2(x).astype(jnp.bfloat16))
            probs = jnp.concatenate(probs, axis=1)
            sums[some] += jnp.dot(probs, values, preferred_element_type=jnp.float32)
        high[...] = highest
        return carry

    for place, of in enumerate(folded):
        lax.fori_loop(0, groups_of(of), functools.partial(fold, of, place), 0)
    if not last:
        return

    unsafe = (jnp.max(high[...]) > 100.0) | (jnp.min(sums[:, width:]) < 2.0**-80)

    @pl.when(unsafe)
    def _():
        sums[...] = jnp.zeros(sums.shape, jnp.float32)
        top[...] = jnp.full(top.shape, masked_low, jnp.float32)
        for of in range(chips):
            fetch(of, 0)

            def fold_top(j, carry):
                keys, hidden, values = group_of(of, 0, j)
                for i in range(0, key_group, 2):
                    x = exponents(keys, hidden, i)
                    before = top[...]
                    after = jnp.maximum(before, jnp.max(x, axis=1, keepdims=True))
                    fade = jnp.exp2(before - after)
                    top[...] = after
                    probs = jnp.exp2(x - jnp.concatenate([after, after], axis=1))
                    sums[...] = sums[...] * jnp.concatenate([fade, fade], axis=1) + jnp.dot(
                        probs.astype(jnp.bfloat16),
                        values[i * BLOCK_TOKENS : (i + 2) * BLOCK_TOKENS],
                        preferred_element_type=jnp.float32,
                    )
                return carry

            lax.fori_loop(0, groups_of(of), fold_top, 0)
        fetch(folded[0], 0)

    for h in range(heads):
        at = slice(h * BLOCK_TOKENS, (h + 1) * BLOCK_TOKENS)
        o_ref[:, h * width : (h + 1) * width] = (sums[at, :width] / sums[at, width:]).astype(
            o_ref.dtype
        )


def attend(folded, tab, pos, q_two, kv_refs, count, part=None, state=None):
    last = state is not None
    state = state or []
    width = q_two[0].shape[2]
    heads = width // HEAD_WIDTH
    rows = heads * BLOCK_TOKENS
    q_spec = pl.BlockSpec(
        (1, BLOCK_TOKENS, width), lambda i, tab, pos: (query_slot(i, pos, part)[0], 0, 0)
    )
    acc_block = (1, rows + 8, 2 * HEAD_WIDTH)

    def acc_spec(whole):
        if whole:
            return pl.BlockSpec(acc_block, lambda i, tab, pos: (query_block(i, pos, part), 0, 0))
        return pl.BlockSpec(acc_block, lambda i, tab, pos: (i + (part[1] if last else 0), 0, 0))

    scratch = [
        pltpu.VMEM((len(folded) * share, BLOCK_TOKENS, 2 * HEAD_WIDTH), jnp.bfloat16),
        pltpu.VMEM((rows, HEAD_WIDTH), jnp.bfloat16),
        pltpu.SemaphoreType.DMA((2 * len(folded),)),
    ]
    if last:
        out_shape = jax.ShapeDtypeStruct((count * BLOCK_TOKENS, width), jnp.bfloat16)
        out_specs = pl.BlockSpec((BLOCK_TOKENS, width), lambda i, *_: (i, 0))
        scratch += [
            pltpu.VMEM((rows + 8, 2 * HEAD_WIDTH), jnp.float32),
            pltpu.VMEM((rows, HEAD_WIDTH), jnp.float32),
        ]
    else:
        out_shape = jax.ShapeDtypeStruct((count, rows + 8, 2 * HEAD_WIDTH), jnp.float32)
        out_specs = acc_spec(part is None)
    shape = (kv_refs[0].shape[0] // BLOCK_TOKENS, BLOCK_TOKENS, kv_refs[0].shape[1])
    work = count * len(folded) * share // 2 * rows * BLOCK_TOKENS
    return pl.pallas_call(
        functools.partial(attend_kernel, folded, part, last, heads),
        out_shape=out_shape,
        grid_spec=pltpu.PrefetchScalarGridSpec(
            num_scalar_prefetch=2,
            grid=(count,),
            in_specs=[q_spec] * 2
            + [pl.BlockSpec(memory_space=pl.ANY)] * len(kv_refs)
            + [acc_spec(whole) for whole, _ in state],
            out_specs=out_specs,
            scratch_shapes=scratch,
        ),
        compiler_params=pltpu.CompilerParams(vmem_limit_bytes=attend_vmem),
        cost_estimate=pl.CostEstimate(
            flops=work * 4 * HEAD_WIDTH * 4, bytes_accessed=work // 8, transcendentals=work
        ),
        name="attend",
    )(tab, pos, *q_two, *[a.reshape(shape) for a in kv_refs], *[a for _, a in state])


def piece_chip(i, z):
    far = jnp.where(z < 2, 2, 1)
    return z ^ i if i < 2 else far ^ (i % 2)


def project_kernel(kinds, held, far, pos, near, *refs):
    sides = len(kinds)
    come, out = refs[:2] if far else (near, near)
    refs = refs[2 * far :]
    w_refs, refs = refs[:sides], refs[sides:]
    bases, refs = refs[: sides * held], refs[sides * held :]
    o_refs, (parts, w_swap, sems, w_sems) = refs[:sides], refs[sides:]
    ends = (pos[0] == 0) | (pos[0] == 3)

    def bring(i, source):
        return pltpu.make_async_copy(source, parts.at[pl.ds(2 * i, 2)], sems.at[i])

    if not held:
        bring(0, near).start()
    if far:

        @pl.when(ends)
        def _():
            bring(1, out).start()

        @pl.when(jnp.logical_not(ends))
        def _():
            bring(1, come).start()

    used = range(2 * held, 4 if far else 2)
    places = [piece_chip(i, pos[0]) for i in range(4)]
    copies = {}
    if "swap" in kinds:
        source = w_refs[kinds.index("swap")]
        for i in used:
            copies[i] = pltpu.make_async_copy(source.at[places[i]], w_swap.at[i], w_sems.at[i])
            copies[i].start()
    for i in range(used.start // 2, used.stop // 2):
        bring(i, near).wait()
    depth = near.shape[2]
    tile = 256
    own_rows = pl.ds(pl.multiple_of(pos[1] * depth, depth), depth)

    for side in sorted(range(sides), key=lambda i: kinds[i] == "swap"):
        if kinds[side] == "swap":
            for i in used:
                copies[i].wait()
        for at in range(0, o_refs[side].shape[1], tile):
            columns = slice(at, at + tile)
            terms = []
            for i in used:
                if kinds[side] == "swap":
                    weight = w_swap[i, :, columns]
                else:
                    weight = w_refs[side][places[i], own_rows, columns]
                terms.append(jnp.dot(parts[i], weight, preferred_element_type=jnp.float32))
            if held:
                terms.append(bases[side][:, columns])
            o_ref = o_refs[side]
            o_ref[:, columns] = functools.reduce(jnp.add, terms).astype(o_ref.dtype)


def project(pos, near, far, weights, types, bases=()):
    vmem = pl.BlockSpec(memory_space=pltpu.VMEM)
    rows, depth = near.shape[1:]
    chips, _, columns = weights[0].shape
    sides = len(weights)
    kinds = tuple("swap" if w.shape[1] == depth else "own" for w in weights)
    places = [pl.BlockSpec(memory_space=pl.ANY) if kind == "swap" else vmem for kind in kinds]
    return pl.pallas_call(
        functools.partial(project_kernel, kinds, bool(bases), bool(far)),
        out_shape=tuple(jax.ShapeDtypeStruct((rows, columns), kind) for kind in types),
        in_specs=[pl.BlockSpec(memory_space=pltpu.SMEM)]
        + [pl.BlockSpec(memory_space=pl.ANY)] * (1 + len(far))
        + places
        + [vmem] * len(bases),
        out_specs=(vmem,) * sides,
        scratch_shapes=[
            pltpu.VMEM((chips, rows, depth), jnp.bfloat16),
            pltpu.VMEM((chips, depth, columns), jnp.bfloat16),
            pltpu.SemaphoreType.DMA((2,)),
            pltpu.SemaphoreType.DMA((chips,)),
        ],
        compiler_params=pltpu.CompilerParams(vmem_limit_bytes=project_vmem),
        cost_estimate=pl.CostEstimate(
            flops=2 * rows * chips * depth * sides * columns,
            bytes_accessed=2 * sides * (chips * depth + 3 * rows) * columns,
            transcendentals=0,
        ),
        name="project",
    )(pos, near, *far, *weights, *bases)


def finish_kernel(own, come, theirs, *refs):
    total = own[...] + come[...].astype(jnp.float32) + theirs[...].astype(jnp.float32)
    refs[-1][...] = total.astype(jnp.bfloat16)


def finish(at, size, own, come, theirs, result=None):
    rows, columns = own.shape
    block = pl.BlockSpec((rows, columns), lambda i: (0, 0))
    held = () if result is None else (result,)
    return pl.pallas_call(
        finish_kernel,
        out_shape=jax.ShapeDtypeStruct((size, columns), jnp.bfloat16),
        grid=(1,),
        in_specs=[block] * 3 + [pl.BlockSpec(memory_space=pl.ANY)] * len(held),
        out_specs=pl.BlockSpec((rows, columns), lambda i: (at, 0)),
        input_output_aliases={3: 0} if held else {},
        compiler_params=pltpu.CompilerParams(vmem_limit_bytes=attend_vmem),
        name="finish",
    )(own, come, theirs, *held)


def apart(k):
    return [(i, i ^ k) for i in range(8)]


def key_lists(meta, blocks):
    chips = meta.shape[0]
    naming = meta[:, :, : 8 * 4].reshape(chips, share, 4)
    fill = meta[:, :, 8 * 4 : 8 * 5].reshape(chips, share)
    wanted = jnp.arange(blocks, dtype=jnp.int32)[None, :, None, None]
    listed = jnp.any(naming[:, None] == wanted, axis=3)
    ones = listed.astype(jnp.int32)
    place = jnp.arange(share, dtype=jnp.int32)
    before = jnp.sum(jnp.where(place[None, :] < place[:, None], ones[:, :, None, :], 0), axis=3)
    entry = place * 256 + fill
    tab = jnp.sum(
        jnp.where(
            listed[..., None] & (before[..., None] == place),
            entry[:, None, :, None],
            0,
        ),
        axis=2,
    )
    return jnp.concatenate([tab, jnp.sum(ones, axis=2, keepdims=True)], axis=2)


def permute(array, perm, axis="tensor"):
    return lax.ppermute(array, axis, perm)


def exchanged_shards(queries, keyvals, attending, block_fill, out_weight):
    t = lax.axis_index("tensor")
    z, core = t // 2, t % 2
    row = lax.axis_index("rows")
    chips = 4
    q_len = queries.shape[0]
    wide = queries.shape[1] // chips
    depth = wide // 2
    pair = 2 * HEAD_WIDTH

    def swap(array):
        return permute(array, apart(1))

    def q_for(chip):
        return lax.dynamic_slice(queries, (0, chip * wide), (q_len, wide))

    def kv_for(chip):
        return lax.dynamic_slice(keyvals, (0, chip * pair), (keyvals.shape[0], pair))

    def columns_of(arrays, which):
        size = (q_len, depth)
        return jnp.stack([lax.dynamic_slice(a, (0, which * depth), size) for a in arrays])

    q_come = [q_for(z)]
    for k in range(1, chips):
        q_come.append(permute(q_for(z ^ k), apart(2 * k)))
    note = jnp.concatenate([attending.reshape(-1), block_fill]).astype(jnp.bfloat16)
    note = jnp.pad(note[None, :], ((0, meta_rows - 1), (0, HEAD_WIDTH - note.shape[0])))
    notes = [note] + [permute(note, apart(2 * k)) for k in range(1, chips)]
    kv = []
    for k in range(chips):
        own = kv_for(z ^ k)
        if k:
            own = permute(own, apart(2 * k))
        kv.append((own, swap(own)))

    q_own = columns_of(q_come, core)
    q_swap = swap(columns_of(q_come, 1 - core))
    q_two = (q_own, q_swap)
    notes = jnp.stack(notes)
    notes = jnp.stack([notes[:, 0, :64], swap(notes)[:, 0, :64]], axis=1)
    tab = key_lists(notes.astype(jnp.int32), 2 * chips)
    pos = jnp.stack([z, core, row]).astype(jnp.int32)
    q_two = (q_own, q_swap)
    whole = [attend((k,), tab, pos, q_two, kv[k], 2 * chips) for k in range(2)]
    half = attend((2,), tab, pos, q_two, kv[2], chips, (False, 0))

    w_own = out_weight.reshape(chips, wide, out_weight.shape[1])
    w_swap = lax.dynamic_slice(
        w_own, (0, (1 - core) * depth, 0), (chips, depth, out_weight.shape[1])
    )
    w_swap = swap(w_swap)
    across = [(2, 4), (3, 5), (4, 2), (5, 3)]
    outward = [(2, 0), (3, 1), (4, 6), (5, 7)]
    every_key = [a for of in kv for a in of]

    def chunk(i, part, count):
        state = [(True, a) for a in whole] + [(False, half)] * (not part[0])
        late = (2, 3) if part[0] else (3,)
        mine = attend(late, tab, pos, q_two, every_key, count, part, state)
        near = jnp.stack([mine, permute(mine, apart(2))])
        come = permute(near, across)
        out = permute(come, outward)
        far = (come, out)
        if i + 1 < len(chunks):
            both = (w_swap, w_own), (jnp.bfloat16, jnp.float32)
            other, own = project(pos, near, far, *both)
        else:
            both = (w_swap, w_own), (jnp.float32, jnp.float32)
            bases = project(pos, near, (), *both)
            (other,) = project(pos, near, far, (w_swap,), (jnp.bfloat16,), bases[:1])
            (own,) = project(pos, near, far, (w_own,), (jnp.float32,), bases[1:])
        return own, swap(other)

    theirs = []
    result = None
    for i, (mine, offset, count) in enumerate(chunks):
        own, come = chunk(i, (mine, offset), count)
        if mine:
            other = theirs[offset // count]
            result = finish(offset // count, q_len * 4, own, come, other, result)
        else:
            sent = (own + come.astype(jnp.float32)).astype(jnp.bfloat16)
            theirs.append(permute(sent, [(0, 1), (1, 0)], "rows"))
    return result


def solution(mesh):
    tensor, rows = mesh.shape["tensor"], mesh.shape["rows"]

    def splits(queries, keyvals):
        return (
            tensor == 8
            and rows == 2
            and keyvals.shape[1] == 4 * 2 * HEAD_WIDTH
            and queries.shape[0] == BLOCK_TOKENS
            and keyvals.shape[0] == 8 * BLOCK_TOKENS
        )

    def shards(queries, keyvals, attending, block_fill, out_weight):
        form = exchanged_shards if splits(queries, keyvals) else gathered_shards
        return form(queries, keyvals, attending, block_fill, out_weight)

    return jax.shard_map(
        shards,
        mesh=mesh,
        in_specs=(
            P(("groups", "tensor"), "rows"),
            P(("groups", "tensor"), "rows"),
            P(("groups", "tensor"), None),
            P(("groups", "tensor")),
            P("rows", "tensor"),
        ),
        out_specs=P(("groups", "rows"), "tensor"),
        check_vma=False,
    )
```
